128 devices in a mesh: left: 16 (over y, z_lo, core), right: 8 (over z_hi, x).
Axes of the slice: x: 4, y: 4, z: 4 (z_hi: 2, z_lo: 2; z = z_hi * 2 + z_lo), core: 2. Of those that a mesh axis runs over, the one named last changes fastest.
Arguments:
- corner: bfloat16 [128, 256, 256], P(('left', 'right')), may hold values from -6 to 6
- edge_row: bfloat16 [256, 64, 256, 256], P('left', 'right'), may hold values from -0.046875 to 0.046875
- source_row: int32 [256, 64], P('left', 'right'), may hold values from 0 to 127, as said below
- proj_row: bfloat16 [256, 256, 256], P('left'), may hold values from -0.375 to 0.375
- edge_col: bfloat16 [32, 160, 256, 256], P('right', 'left'), may hold values from -0.03125 to 0.03125
- source_col: int32 [32, 160], P('right', 'left'), may hold values from 0 to 255, as said below
- proj_col: bfloat16 [32, 256, 256], P('right'), may hold values from -0.375 to 0.375
Outputs:
- absorbed_row: bfloat16 [256, 256, 256], P(('left', 'right'))
- new_corner: bfloat16 [32, 256, 256], P('right', 'left')
The draws below stay inside these ranges and needn't reach their ends.
Inputs may be any that keep to these rules, and one draw needn't show every extreme that they name: source_row[f, j] is a sector whose block lies on a device with right index j // 8, that is (source_row[f, j]) % 8 == j // 8. source_col[g, j] is a sector of the left index j // 10: source_col[g, j] // 16 == j // 10.
All inputs are finite; a program needn't handle non-finite values.
Results may differ from the reference program's by a relative error of at most 0.03.
Values may be sent and summed in bfloat16 or wider, within the bound.
No kernel may reach another device: no remote copies, remote signals or barrier semaphores. Data moves between devices by JAX's collectives and lax.ppermute only.
A program may use at most 128 MiB of HBM per device.

```python
import jax
import jax.numpy as jnp
from jax import lax

P_SIZE = 256
SEC_DEV = 1
O1 = 2
K1 = 8
K2 = 10
NSEC = 128
NOUT1 = 256
KF1 = 64
NOUT2 = 32
KF2 = 160
N_LEFT = 16
N_RIGHT = 8


def draw_source_row(key, part):
    key_left = jax.random.fold_in(key, 11)
    key_local = jax.random.fold_in(key, 12)
    left_pick = jax.random.randint(key_left, (NOUT1, KF1), 0, N_LEFT)
    local_pick = jax.random.randint(key_local, (NOUT1, KF1), 0, SEC_DEV)
    right_owner = (jnp.arange(KF1, dtype=jnp.int32) // K1)[None, :]
    values = left_pick * (N_RIGHT * SEC_DEV) + right_owner * SEC_DEV + local_pick
    values = values.at[0, 0].set(0)
    values = values.at[NOUT1 - 1, KF1 - 1].set(NSEC - 1)
    return values.astype(jnp.int32)


def draw_source_col(key, part):
    key_pick = jax.random.fold_in(key, 21)
    inner_pick = jax.random.randint(key_pick, (NOUT2, KF2), 0, O1 * N_RIGHT)
    left_owner = (jnp.arange(KF2, dtype=jnp.int32) // K2)[None, :]
    values = left_owner * (O1 * N_RIGHT) + inner_pick
    values = values.at[0, 0].set(0)
    values = values.at[NOUT2 - 1, KF2 - 1].set(NOUT1 - 1)
    return values.astype(jnp.int32)


def levels(stream_key, dims, shards, smallest, top_value):
    factor_of, own = 1.0, jax.random.fold_in(stream_key, 6)
    for dim, parts in shards:
        steps = jnp.exp(jax.random.uniform(jax.random.fold_in(own, dim), (parts,), jnp.float32, smallest / len(shards), top_value / len(shards)))
        factor_of = factor_of * jnp.repeat(steps, dims[dim] // parts).reshape([-1 if axis == dim else 1 for axis in range(len(dims))])
    return factor_of


def normal_values(stream_key, shape, deviation, most, pieces=(), held_as=jnp.bfloat16):
    level = levels(stream_key, shape, pieces, -0.22, 0.18) if pieces else 1.0
    values = jax.random.normal(stream_key, shape, jnp.float32) * deviation * level
    return jnp.minimum(jnp.maximum(values, -most), most).astype(held_as)


def setup_inputs(seed: int = 0) -> dict:
    key_list = jax.random.split(jax.random.key(seed), 8)
    corner = normal_values(key_list[0], (NSEC, P_SIZE, P_SIZE), 1.0, 6.0, ((0, 128),))
    edge_row = normal_values(key_list[1], (NOUT1, KF1, P_SIZE, P_SIZE), (P_SIZE * KF1) ** -0.5, 0.046875, ((0, 16), (1, 8)))
    source_row = draw_source_row(jax.random.fold_in(key_list[7], 71), 0)
    proj_row = normal_values(key_list[3], (NOUT1, P_SIZE, P_SIZE), P_SIZE ** -0.5, 0.375, ((0, 16),))
    edge_col = normal_values(key_list[4], (NOUT2, KF2, P_SIZE, P_SIZE), (P_SIZE * KF2) ** -0.5, 0.03125, ((0, 8), (1, 16)))
    source_col = draw_source_col(jax.random.fold_in(key_list[7], 71), 0)
    proj_col = normal_values(key_list[6], (NOUT2, P_SIZE, P_SIZE), P_SIZE ** -0.5, 0.375, ((0, 8),))
    return dict(corner=corner, edge_row=edge_row, source_row=source_row, proj_row=proj_row, edge_col=edge_col, source_col=source_col, proj_col=proj_col)


def reference(corner, edge_row, source_row, proj_row, edge_col, source_col, proj_col):
    def row_one(items):
        index_list, edges, projector = items
        blocks = jnp.take(corner, index_list, axis=0).astype(jnp.float32)
        row_sum = jnp.einsum("kab,kbc->ac", blocks, edges.astype(jnp.float32)).astype(jnp.bfloat16)
        return jnp.dot(projector.T, row_sum, preferred_element_type=jnp.float32).astype(jnp.bfloat16)

    absorbed_row = lax.map(row_one, (source_row, edge_row, proj_row))

    def col_one(items):
        index_list, edges, projector = items
        blocks = jnp.take(absorbed_row, index_list, axis=0).astype(jnp.float32)
        col_sum = jnp.einsum("kab,kbc->ac", edges.astype(jnp.float32), blocks).astype(jnp.bfloat16)
        return jnp.dot(col_sum, projector, preferred_element_type=jnp.float32).astype(jnp.bfloat16)

    new_corner = lax.map(col_one, (source_col, edge_col, proj_col))
    return absorbed_row, new_corner
```

```python
import jax
import jax.numpy as jnp
from jax import lax
from jax.experimental import pallas as pl
from jax.experimental.pallas import tpu as pltpu
from jax.sharding import PartitionSpec as P

F32 = jnp.float32
BF16 = jnp.bfloat16
SIZE = 256


def row_kernel(slot_ref, own_ref, other_ref, edge_ref, out_ref, held, sems):
    step = pl.program_id(0)
    half = own_ref.shape[0]

    @pl.when(step == 0)
    def _():
        first = pltpu.make_async_copy(own_ref, held.at[pl.ds(0, half)], sems.at[0])
        second = pltpu.make_async_copy(other_ref, held.at[pl.ds(half, half)], sems.at[1])
        first.start()
        second.start()
        first.wait()
        second.wait()

    total = jnp.dot(held[slot_ref[step, 0]], edge_ref[0, 0], preferred_element_type=F32)
    for entry in range(1, edge_ref.shape[1]):
        total += jnp.dot(held[slot_ref[step, entry]], edge_ref[0, entry], preferred_element_type=F32)
    out_ref[0] = total.astype(BF16)


def row_partial(slots, own, other, edge_row):
    sectors, entries = edge_row.shape[:2]
    half = own.shape[0]
    return pl.pallas_call(
        row_kernel,
        out_shape=jax.ShapeDtypeStruct((sectors, SIZE, SIZE), BF16),
        grid_spec=pltpu.PrefetchScalarGridSpec(
            num_scalar_prefetch=1,
            grid=(sectors,),
            in_specs=[
                pl.BlockSpec(memory_space=pl.ANY),
                pl.BlockSpec(memory_space=pl.ANY),
                pl.BlockSpec((1, entries, SIZE, SIZE), lambda f, s: (f, 0, 0, 0)),
            ],
            out_specs=pl.BlockSpec((1, SIZE, SIZE), lambda f, s: (f, 0, 0)),
            scratch_shapes=[
                pltpu.VMEM((2 * half, SIZE, SIZE), BF16),
                pltpu.SemaphoreType.DMA((2,)),
            ],
        ),
        compiler_params=pltpu.CompilerParams(vmem_limit_bytes=24 * 2**20),
        name="row_partial",
    )(slots, own, other, edge_row)


def absorb_kernel(first_ref, part_ref, proj_ref, mine_ref, copies_ref):
    total = jnp.sum(part_ref[:, 0].astype(F32), axis=0).astype(BF16)
    value = lax.dot_general(
        proj_ref[0], total, (((0,), (0,)), ((), ())), preferred_element_type=F32
    ).astype(BF16)
    mine_ref[0] = value
    for peer in range(copies_ref.shape[0]):
        copies_ref[peer, 0] = value


def absorb(first, parts, proj_row):
    peers, held = parts.shape[:2]
    return pl.pallas_call(
        absorb_kernel,
        out_shape=(
            jax.ShapeDtypeStruct((held, SIZE, SIZE), BF16),
            jax.ShapeDtypeStruct((peers, held, SIZE, SIZE), BF16),
        ),
        grid_spec=pltpu.PrefetchScalarGridSpec(
            num_scalar_prefetch=1,
            grid=(held,),
            in_specs=[
                pl.BlockSpec((peers, 1, SIZE, SIZE), lambda f, s: (0, f, 0, 0)),
                pl.BlockSpec((1, SIZE, SIZE), lambda f, s: (s[0] + f, 0, 0)),
            ],
            out_specs=(
                pl.BlockSpec((1, SIZE, SIZE), lambda f, s: (f, 0, 0)),
                pl.BlockSpec((peers, 1, SIZE, SIZE), lambda f, s: (0, f, 0, 0)),
            ),
        ),
        name="absorb",
    )(first, parts, proj_row)


def col_kernel(slot_ref, rows_ref, edge_ref, out_ref):
    step = pl.program_id(0)
    total = jnp.dot(edge_ref[0, 0], rows_ref[slot_ref[step, 0]], preferred_element_type=F32)
    for entry in range(1, edge_ref.shape[1]):
        total += jnp.dot(edge_ref[0, entry], rows_ref[slot_ref[step, entry]], preferred_element_type=F32)
    out_ref[:, 0] = total.astype(BF16).reshape(out_ref.shape[0], out_ref.shape[2], SIZE)


def col_partial(slots, rows, edge_col, pieces):
    sectors, entries = edge_col.shape[:2]
    piece = SIZE // pieces
    return pl.pallas_call(
        col_kernel,
        out_shape=jax.ShapeDtypeStruct((pieces, sectors, piece, SIZE), BF16),
        grid_spec=pltpu.PrefetchScalarGridSpec(
            num_scalar_prefetch=1,
            grid=(sectors,),
            in_specs=[
                pl.BlockSpec(rows.shape, lambda g, s: (0, 0, 0), pipeline_mode=pl.Buffered(1)),
                pl.BlockSpec((1, entries, SIZE, SIZE), lambda g, s: (g, 0, 0, 0)),
            ],
            out_specs=pl.BlockSpec((pieces, 1, piece, SIZE), lambda g, s: (0, g, 0, 0)),
        ),
        compiler_params=pltpu.CompilerParams(vmem_limit_bytes=24 * 2**20),
        name="col_partial",
    )(slots, rows, edge_col)


def finish_kernel(part_ref, proj_ref, out_ref):
    for sector in range(proj_ref.shape[0]):
        total = jnp.sum(part_ref[:, sector].astype(F32), axis=0).astype(BF16)
        out_ref[sector] = jnp.dot(total, proj_ref[sector], preferred_element_type=F32).astype(BF16)


def finish(parts, proj_col):
    _, sectors, piece, _ = parts.shape
    return pl.pallas_call(
        finish_kernel,
        out_shape=jax.ShapeDtypeStruct((sectors, piece, SIZE), BF16),
        name="finish",
    )(parts, proj_col)


def body(corner, edge_row, source_row, proj_row, edge_col, source_col, proj_col):
    lefts, rights = lax.axis_size("left"), lax.axis_size("right")
    left, right = lax.axis_index("left"), lax.axis_index("right")

    parity = [list(range(start, lefts, 2)) for start in range(2)]
    own = lax.all_to_all(
        jnp.broadcast_to(corner, (lefts // 2, SIZE, SIZE)), "left", 0, 0, axis_index_groups=parity, tiled=True
    )
    other = lax.ppermute(own, "left", [(i, i ^ 1) for i in range(lefts)])
    owner = source_row // rights
    slots = owner // 2 + jnp.where(owner % 2 == left % 2, 0, lefts // 2)
    partial_rows = row_partial(slots, own, other, edge_row)

    sectors = edge_row.shape[0]
    held = sectors // rights
    parts = lax.all_to_all(partial_rows.reshape(rights, held, SIZE, SIZE), "right", 0, 0, tiled=True)
    first = jnp.reshape(right * held, (1,)).astype(jnp.int32)
    absorbed, copies = absorb(first, parts, proj_row)
    rows = lax.all_to_all(copies, "right", 0, 0, tiled=True).reshape(sectors, SIZE, SIZE)

    partial_cols = col_partial(source_col - left * sectors, rows, edge_col, lefts)
    col_parts = lax.all_to_all(partial_cols, "left", 0, 0, tiled=True)
    return absorbed, finish(col_parts, proj_col)


def solution(mesh):
    in_specs = (
        P(("left", "right"), None, None),
        P("left", "right", None, None),
        P("left", "right"),
        P("left", None, None),
        P("right", "left", None, None),
        P("right", "left"),
        P("right", None, None),
    )
    out_specs = (P(("left", "right"), None, None), P("right", "left", None))
    return jax.shard_map(body, mesh=mesh, in_specs=in_specs, out_specs=out_specs, check_vma=False)
```

```python
import jax
import jax.numpy as jnp
from jax import lax
from jax.experimental import pallas as pl
from jax.experimental.pallas import tpu as pltpu
from jax.sharding import PartitionSpec as P

F32 = jnp.float32
BF16 = jnp.bfloat16
SIZE = 256
COUNT = 2
FLAT = COUNT * SIZE
FLIPS = (1, 3, 4)
ORDERS = ((0, 1, 2), (1, 2, 0), (2, 0, 1))
CUTS = (0, 176, 352, FLAT)
LENGTHS = tuple(CUTS[i + 1] - CUTS[i] for i in range(3))
VMEM = pl.BlockSpec(memory_space=pltpu.VMEM)
SMALL = pltpu.CompilerParams(vmem_limit_bytes=8 * 2**20)


def flip(value, pairing, size):
    return lax.ppermute(value, "right", [(i, i ^ FLIPS[pairing]) for i in range(size)])


def place_of(place, order):
    bits = [place // 4, place // 2 % 2, place % 2]
    return bits[order[0]] * 4 + bits[order[1]] * 2 + bits[order[2]]


def cost(flops, elements):
    return pl.CostEstimate(flops=flops, bytes_accessed=2 * elements, transcendentals=0)


def row_kernel(slot_ref, peer_ref, held_ref, edge_ref, *out_refs):
    step = pl.program_id(0)
    place = pl.num_programs(0) - 1 - step
    first = peer_ref[step] * COUNT
    values = []
    for sector in range(COUNT):
        total = jnp.dot(held_ref[slot_ref[first + sector, 0]], edge_ref[sector, 0], preferred_element_type=F32)
        for entry in range(1, edge_ref.shape[1]):
            total += jnp.dot(
                held_ref[slot_ref[first + sector, entry]], edge_ref[sector, entry], preferred_element_type=F32
            )
        values.append(total)
    flat = jnp.concatenate(values, axis=0)
    for part, order in enumerate(ORDERS):
        index = place_of(place, order)
        send_ref, keep_ref = out_refs[2 * part], out_refs[2 * part + 1]
        value = flat[CUTS[part] : CUTS[part + 1]]

        @pl.when(index >= 4)
        def _():
            send_ref[index - 4] = value.astype(BF16)

        @pl.when(index < 4)
        def _():
            keep_ref[index] = value


def row_partial(slots, peers, held, edge_row):
    entries = edge_row.shape[1]
    steps = peers.shape[0]
    outs = []
    for length in LENGTHS:
        outs.append(jax.ShapeDtypeStruct((steps // 2, length, SIZE), BF16))
        outs.append(jax.ShapeDtypeStruct((steps // 2, length, SIZE), F32))
    return pl.pallas_call(
        row_kernel,
        out_shape=tuple(outs),
        grid_spec=pltpu.PrefetchScalarGridSpec(
            num_scalar_prefetch=2,
            grid=(steps,),
            in_specs=[
                VMEM,
                pl.BlockSpec((COUNT, entries, SIZE, SIZE), lambda s, slots, peers: (peers[s], 0, 0, 0)),
            ],
            out_specs=tuple(VMEM for _ in outs),
        ),
        compiler_params=pltpu.CompilerParams(vmem_limit_bytes=24 * 2**20),
        cost_estimate=cost(2 * steps * COUNT * entries * SIZE**3, steps * COUNT * entries * SIZE**2),
        name="row_partial",
    )(slots, peers, held, pltpu.with_memory_space_constraint(edge_row, pltpu.HBM))


def halve_kernel(*refs):
    for part in range(3):
        keep_ref, came_ref = refs[2 * part], refs[2 * part + 1]
        send_ref, rest_ref = refs[6 + 2 * part], refs[7 + 2 * part]
        half = send_ref.shape[0]
        send_ref[...] = (keep_ref[half:] + came_ref[half:].astype(F32)).astype(BF16)
        rest_ref[...] = keep_ref[:half] + came_ref[:half].astype(F32)


def halve(keeps, came):
    half = keeps[0].shape[0] // 2
    outs = []
    for length in LENGTHS:
        outs.append(jax.ShapeDtypeStruct((half, length, SIZE), BF16))
        outs.append(jax.ShapeDtypeStruct((half, length, SIZE), F32))
    args = [value for pair in zip(keeps, came) for value in pair]
    return pl.pallas_call(
        halve_kernel,
        out_shape=tuple(outs),
        in_specs=[VMEM] * 6,
        out_specs=tuple(VMEM for _ in outs),
        compiler_params=SMALL,
        cost_estimate=cost(4 * half * FLAT * SIZE, 6 * half * FLAT * SIZE),
        name="halve",
    )(*args)


def absorb_kernel(proj_ref, *refs):
    keep_refs, came_refs, out_ref, part_refs = refs[:3], refs[3:6], refs[6], refs[7:]
    pieces = [keep[0] + came[0].astype(F32) for keep, came in zip(keep_refs, came_refs)]
    total = jnp.concatenate(pieces, axis=0).astype(BF16)
    values = []
    for sector in range(COUNT):
        value = lax.dot_general(
            proj_ref[sector],
            total[sector * SIZE : (sector + 1) * SIZE],
            (((0,), (0,)), ((), ())),
            preferred_element_type=F32,
        ).astype(BF16)
        out_ref[sector] = value
        values.append(value)
    flat = jnp.concatenate(values, axis=0)
    for part, part_ref in enumerate(part_refs):
        part_ref[0] = flat[CUTS[part] : CUTS[part + 1]]


def absorb(index, keeps, came, proj_row):
    outs = [jax.ShapeDtypeStruct((COUNT, SIZE, SIZE), BF16)]
    outs += [jax.ShapeDtypeStruct((1, length, SIZE), BF16) for length in LENGTHS]
    return pl.pallas_call(
        lambda index_ref, *refs: absorb_kernel(*refs),
        out_shape=tuple(outs),
        grid_spec=pltpu.PrefetchScalarGridSpec(
            num_scalar_prefetch=1,
            grid=(1,),
            in_specs=[pl.BlockSpec((COUNT, SIZE, SIZE), lambda s, index: (index[0], 0, 0))] + [VMEM] * 6,
            out_specs=tuple(VMEM for _ in outs),
        ),
        compiler_params=SMALL,
        cost_estimate=cost(2 * COUNT * SIZE**3, 6 * FLAT * SIZE),
        name="absorb",
    )(index, proj_row, *keeps, *came)


def double_kernel(*refs):
    for part in range(3):
        held_ref, came_ref, out_ref = refs[2 * part], refs[2 * part + 1], refs[6 + part]
        half = held_ref.shape[0]
        out_ref[:half] = held_ref[...]
        out_ref[half:] = came_ref[...]


def double(held, came):
    half = held[0].shape[0]
    args = [value for pair in zip(held, came) for value in pair]
    return pl.pallas_call(
        double_kernel,
        out_shape=tuple(jax.ShapeDtypeStruct((2 * half, length, SIZE), BF16) for length in LENGTHS),
        in_specs=[VMEM] * 6,
        out_specs=tuple(VMEM for _ in range(3)),
        compiler_params=SMALL,
        cost_estimate=cost(0, 4 * half * FLAT * SIZE),
        name="double",
    )(*args)


def col_kernel(slot_ref, *refs):
    piece_refs, (edge_ref, out_ref, held, sems) = refs[:6], refs[6:]
    step = pl.program_id(0)

    @pl.when(step == 0)
    def _():
        copies = []
        for part, order in enumerate(ORDERS):
            for place in range(8):
                index = place_of(place, order)
                source = piece_refs[2 * part + index // 4].at[index % 4]
                target = held.at[pl.ds(place * FLAT + CUTS[part], LENGTHS[part])]
                copies.append(pltpu.make_async_copy(source, target, sems.at[part * 8 + place]))
        for copy in copies:
            copy.start()
        for copy in copies:
            copy.wait()

    def block(entry):
        return held[pl.ds(pl.multiple_of(slot_ref[step, entry] * SIZE, SIZE), SIZE)]

    total = jnp.dot(edge_ref[0, 0], block(0), preferred_element_type=F32)
    for entry in range(1, edge_ref.shape[1]):
        total += jnp.dot(edge_ref[0, entry], block(entry), preferred_element_type=F32)
    out_ref[:, 0] = total.astype(BF16).reshape(out_ref.shape[0], out_ref.shape[2], SIZE)


def col_partial(slots, pieces_in, edge_col, pieces):
    sectors, entries = edge_col.shape[:2]
    piece = SIZE // pieces
    return pl.pallas_call(
        col_kernel,
        out_shape=jax.ShapeDtypeStruct((pieces, sectors, piece, SIZE), BF16),
        grid_spec=pltpu.PrefetchScalarGridSpec(
            num_scalar_prefetch=1,
            grid=(sectors,),
            in_specs=[VMEM] * 6 + [pl.BlockSpec((1, entries, SIZE, SIZE), lambda g, s: (g, 0, 0, 0))],
            out_specs=pl.BlockSpec((pieces, 1, piece, SIZE), lambda g, s: (0, g, 0, 0)),
            scratch_shapes=[pltpu.VMEM((8 * FLAT, SIZE), BF16), pltpu.SemaphoreType.DMA((24,))],
        ),
        compiler_params=pltpu.CompilerParams(vmem_limit_bytes=24 * 2**20),
        cost_estimate=cost(2 * sectors * entries * SIZE**3, sectors * entries * SIZE**2),
        name="col_partial",
    )(slots, *pieces_in, pltpu.with_memory_space_constraint(edge_col, pltpu.HBM))


def finish_kernel(part_ref, proj_ref, out_ref):
    for sector in range(proj_ref.shape[0]):
        total = jnp.sum(part_ref[:, sector].astype(F32), axis=0).astype(BF16)
        out_ref[sector] = jnp.dot(total, proj_ref[sector], preferred_element_type=F32).astype(BF16)


def finish(parts, proj_col):
    _, sectors, piece, _ = parts.shape
    return pl.pallas_call(
        finish_kernel,
        out_shape=jax.ShapeDtypeStruct((sectors, piece, SIZE), BF16),
        in_specs=[VMEM] * 2,
        compiler_params=SMALL,
        name="finish",
    )(parts, proj_col)


def body(corner, edge_row, source_row, proj_row, edge_col, source_col, proj_col):
    lefts, rights = lax.axis_size("left"), lax.axis_size("right")
    left, right = lax.axis_index("left"), lax.axis_index("right")

    parity = [list(range(start, lefts, 2)) for start in range(2)]
    own = lax.all_to_all(
        jnp.broadcast_to(corner, (lefts // 2, SIZE, SIZE)), "left", 0, 0, axis_index_groups=parity, tiled=True
    )
    other = lax.ppermute(own, "left", [(i, i ^ 1) for i in range(lefts)])
    held = jnp.concatenate([own, other], axis=0)
    source = source_row // rights
    slots = source // 2 + jnp.where(source % 2 == left % 2, 0, lefts // 2)

    offsets = [p * FLIPS[0] ^ q * FLIPS[1] ^ z * FLIPS[2] for p in range(2) for q in range(2) for z in range(2)]
    peers = jnp.bitwise_xor(right, jnp.array(offsets[::-1], jnp.int32))
    outs = row_partial(slots, peers, held, edge_row)
    for phase in range(3):
        came = [flip(outs[2 * part], ORDERS[part][phase], rights) for part in range(3)]
        keeps = outs[1::2]
        if phase < 2:
            outs = halve(keeps, came)
    absorbed, *parts = absorb(jnp.reshape(right, (1,)).astype(jnp.int32), keeps, came, proj_row)

    for phase in range(3):
        came = [flip(parts[part], ORDERS[part][2 - phase], rights) for part in range(3)]
        if phase < 2:
            parts = double(parts, came)
    pieces = [value for pair in zip(parts, came) for value in pair]

    inner = source_col - left * (rights * COUNT)
    offset = jnp.bitwise_xor(inner // COUNT, right)
    z = offset // 4
    q = offset // 2 % 2
    p = (offset + q) % 2
    partial_cols = col_partial((p * 4 + q * 2 + z) * COUNT + inner % COUNT, pieces, edge_col, lefts)
    col_parts = lax.all_to_all(partial_cols, "left", 0, 0, tiled=True)
    return absorbed, finish(col_parts, proj_col)


def solution(mesh):
    in_specs = (
        P(("left", "right"), None, None),
        P("left", "right", None, None),
        P("left", "right"),
        P("left", None, None),
        P("right", "left", None, None),
        P("right", "left"),
        P("right", None, None),
    )
    out_specs = (P(("left", "right"), None, None), P("right", "left", None))
    return jax.shard_map(body, mesh=mesh, in_specs=in_specs, out_specs=out_specs, check_vma=False)
```

```python
import jax
import jax.numpy as jnp
from jax import lax
from jax.experimental import pallas as pl
from jax.experimental.pallas import tpu as pltpu
from jax.sharding import PartitionSpec as P

F32 = jnp.float32
BF16 = jnp.bfloat16
SIZE = 256
COUNT = 2
FLAT = COUNT * SIZE
DEPTH = 4
FLIPS = (1, 3, 4)
ORDERS = ((0, 1, 2), (1, 2, 0), (2, 0, 1))
CUTS = (0, 176, 352, FLAT)
LENGTHS = tuple(CUTS[i + 1] - CUTS[i] for i in range(3))
VMEM = pl.BlockSpec(memory_space=pltpu.VMEM)
SMALL = pltpu.CompilerParams(vmem_limit_bytes=8 * 2**20)


def flip(value, pairing, size):
    return lax.ppermute(value, "right", [(i, i ^ FLIPS[pairing]) for i in range(size)])


def place_of(place, order):
    bits = [place // 4, place // 2 % 2, place % 2]
    return bits[order[0]] * 4 + bits[order[1]] * 2 + bits[order[2]]


def cost(flops, elements):
    return pl.CostEstimate(flops=flops, bytes_accessed=2 * elements, transcendentals=0)


def row_kernel(slot_ref, peer_ref, held_ref, edge_hbm, *refs):
    *out_refs, ring, sems = refs
    step, steps, depth = pl.program_id(0), pl.num_programs(0), ring.shape[0]
    place = steps - 1 - step
    first = peer_ref[step] * COUNT

    def fetch(later):
        slot = later % depth
        return [
            pltpu.make_async_copy(edge_hbm.at[peer_ref[later] * COUNT + i], ring.at[slot, i], sems.at[slot, i])
            for i in range(COUNT)
        ]

    @pl.when(step == 0)
    def _():
        for later in range(depth - 1):
            for copy in fetch(later):
                copy.start()

    @pl.when(step + depth - 1 < steps)
    def _():
        for copy in fetch(step + depth - 1):
            copy.start()

    for copy in fetch(step):
        copy.wait()
    edge_ref = ring.at[step % depth]
    values = []
    for sector in range(COUNT):
        total = jnp.dot(held_ref[slot_ref[first + sector, 0]], edge_ref[sector, 0], preferred_element_type=F32)
        for entry in range(1, edge_ref.shape[1]):
            total += jnp.dot(
                held_ref[slot_ref[first + sector, entry]], edge_ref[sector, entry], preferred_element_type=F32
            )
        values.append(total.T)
    flat = jnp.concatenate(values, axis=0)
    for part, order in enumerate(ORDERS):
        index = place_of(place, order)
        send_ref, keep_ref = out_refs[2 * part], out_refs[2 * part + 1]
        value = flat[CUTS[part] : CUTS[part + 1]]

        @pl.when(index >= 4)
        def _():
            send_ref[index - 4] = value.astype(BF16)

        @pl.when(index < 4)
        def _():
            keep_ref[index] = value


def row_partial(slots, peers, held, edge_row):
    entries = edge_row.shape[1]
    steps = peers.shape[0]
    outs = []
    for length in LENGTHS:
        outs.append(jax.ShapeDtypeStruct((steps // 2, length, SIZE), BF16))
        outs.append(jax.ShapeDtypeStruct((steps // 2, length, SIZE), F32))
    return pl.pallas_call(
        row_kernel,
        out_shape=tuple(outs),
        grid_spec=pltpu.PrefetchScalarGridSpec(
            num_scalar_prefetch=2,
            grid=(steps,),
            in_specs=[VMEM, pl.BlockSpec(memory_space=pl.ANY)],
            out_specs=tuple(VMEM for _ in outs),
            scratch_shapes=[
                pltpu.VMEM((DEPTH, COUNT, entries, SIZE, SIZE), BF16),
                pltpu.SemaphoreType.DMA((DEPTH, COUNT)),
            ],
        ),
        compiler_params=pltpu.CompilerParams(vmem_limit_bytes=24 * 2**20),
        cost_estimate=cost(2 * steps * COUNT * entries * SIZE**3, steps * COUNT * entries * SIZE**2),
        name="row_partial",
    )(slots, peers, held, pltpu.with_memory_space_constraint(edge_row, pltpu.HBM))


def halve_kernel(*refs):
    for part in range(3):
        keep_ref, came_ref = refs[2 * part], refs[2 * part + 1]
        send_ref, rest_ref = refs[6 + 2 * part], refs[7 + 2 * part]
        half = send_ref.shape[0]
        send_ref[...] = (keep_ref[half:] + came_ref[half:].astype(F32)).astype(BF16)
        rest_ref[...] = keep_ref[:half] + came_ref[:half].astype(F32)


def halve(keeps, came):
    half = keeps[0].shape[0] // 2
    outs = []
    for length in LENGTHS:
        outs.append(jax.ShapeDtypeStruct((half, length, SIZE), BF16))
        outs.append(jax.ShapeDtypeStruct((half, length, SIZE), F32))
    args = [value for pair in zip(keeps, came) for value in pair]
    return pl.pallas_call(
        halve_kernel,
        out_shape=tuple(outs),
        in_specs=[VMEM] * 6,
        out_specs=tuple(VMEM for _ in outs),
        compiler_params=SMALL,
        cost_estimate=cost(4 * half * FLAT * SIZE, 6 * half * FLAT * SIZE),
        name="halve",
    )(*args)


def meet_kernel(*refs):
    for part in range(3):
        keep_ref, came_ref, out_ref = refs[2 * part], refs[2 * part + 1], refs[6 + part]
        out_ref[...] = (keep_ref[...] + came_ref[...].astype(F32)).astype(BF16)


def meet(keeps, came):
    args = [value for pair in zip(keeps, came) for value in pair]
    return pl.pallas_call(
        meet_kernel,
        out_shape=tuple(jax.ShapeDtypeStruct(value.shape, BF16) for value in keeps),
        in_specs=[VMEM] * 6,
        out_specs=tuple(VMEM for _ in range(3)),
        compiler_params=SMALL,
        cost_estimate=cost(2 * FLAT * SIZE, 8 * FLAT * SIZE),
        name="meet",
    )(*args)


def absorb_kernel(index_ref, proj_ref, *refs):
    ours_refs, came_refs, out_ref, part_refs = refs[:3], refs[3:6], refs[6], refs[7:]
    mine = []
    for part, order in enumerate(ORDERS):
        low, high = CUTS[part], CUTS[part + 1]
        for place in range(2):
            first = (index_ref[0] ^ (place * FLIPS[order[2]])) * COUNT
            total = (ours_refs[part][place].astype(F32) + came_refs[part][1 - place].astype(F32)).astype(BF16)
            pieces = []
            for sector in range(COUNT):
                start, stop = max(low, sector * SIZE), min(high, (sector + 1) * SIZE)
                if start < stop:
                    pieces.append(
                        jnp.dot(total[start - low : stop - low], proj_ref[first + sector], preferred_element_type=F32)
                    )
            value = jnp.concatenate(pieces, axis=0).astype(BF16)
            part_refs[part][place] = value
            if place == 0:
                mine.append(value)
    flat = jnp.concatenate(mine, axis=0)
    for sector in range(COUNT):
        out_ref[sector] = flat[sector * SIZE : (sector + 1) * SIZE].T


def absorb(index, ours, came, proj_row):
    outs = [jax.ShapeDtypeStruct((COUNT, SIZE, SIZE), BF16)]
    outs += [jax.ShapeDtypeStruct((2, length, SIZE), BF16) for length in LENGTHS]
    return pl.pallas_call(
        absorb_kernel,
        out_shape=tuple(outs),
        in_specs=[pl.BlockSpec(memory_space=pltpu.SMEM)] + [VMEM] * 7,
        out_specs=tuple(VMEM for _ in outs),
        compiler_params=SMALL,
        cost_estimate=cost(4 * COUNT * SIZE**3, 10 * FLAT * SIZE),
        name="absorb",
    )(index, proj_row, *ours, *came)


def double_kernel(*refs):
    for part in range(3):
        held_ref, came_ref, out_ref = refs[2 * part], refs[2 * part + 1], refs[6 + part]
        half = held_ref.shape[0]
        out_ref[:half] = held_ref[...]
        out_ref[half:] = came_ref[...]


def double(held, came):
    half = held[0].shape[0]
    args = [value for pair in zip(held, came) for value in pair]
    return pl.pallas_call(
        double_kernel,
        out_shape=tuple(jax.ShapeDtypeStruct((2 * half, length, SIZE), BF16) for length in LENGTHS),
        in_specs=[VMEM] * 6,
        out_specs=tuple(VMEM for _ in range(3)),
        compiler_params=SMALL,
        cost_estimate=cost(0, 4 * half * FLAT * SIZE),
        name="double",
    )(*args)


def col_kernel(slot_ref, *refs):
    piece_refs, (edge_hbm, out_ref, held, edge_ref, edge_sems) = refs[:6], refs[6:]
    step = pl.program_id(0)

    def fetch(later):
        return pltpu.make_async_copy(edge_hbm.at[later], edge_ref.at[later], edge_sems.at[later])

    @pl.when(step == 0)
    def _():
        for later in range(edge_ref.shape[0]):
            fetch(later).start()
        for part, order in enumerate(ORDERS):
            for place in range(8):
                index = place_of(place, order)
                start = place * FLAT + CUTS[part]
                held[start : start + LENGTHS[part]] = piece_refs[2 * part + index // 4][index % 4]

    fetch(step).wait()

    def block(entry):
        return held[pl.ds(pl.multiple_of(slot_ref[step, entry] * SIZE, SIZE), SIZE)]

    def term(entry):
        return lax.dot_general(
            edge_ref[step, entry], block(entry), (((1,), (1,)), ((), ())), preferred_element_type=F32
        )

    total = term(0)
    for entry in range(1, edge_ref.shape[1]):
        total += term(entry)
    out_ref[:, 0] = total.astype(BF16).reshape(out_ref.shape[0], out_ref.shape[2], SIZE)


def col_partial(slots, pieces_in, edge_col, pieces):
    sectors, entries = edge_col.shape[:2]
    piece = SIZE // pieces
    return pl.pallas_call(
        col_kernel,
        out_shape=jax.ShapeDtypeStruct((pieces, sectors, piece, SIZE), BF16),
        grid_spec=pltpu.PrefetchScalarGridSpec(
            num_scalar_prefetch=1,
            grid=(sectors,),
            in_specs=[VMEM] * 6 + [pl.BlockSpec(memory_space=pl.ANY)],
            out_specs=pl.BlockSpec((pieces, 1, piece, SIZE), lambda g, s: (0, g, 0, 0)),
            scratch_shapes=[
                pltpu.VMEM((8 * FLAT, SIZE), BF16),
                pltpu.VMEM(edge_col.shape, BF16),
                pltpu.SemaphoreType.DMA((sectors,)),
            ],
        ),
        compiler_params=pltpu.CompilerParams(vmem_limit_bytes=24 * 2**20),
        cost_estimate=cost(2 * sectors * entries * SIZE**3, sectors * entries * SIZE**2),
        name="col_partial",
    )(slots, *pieces_in, pltpu.with_memory_space_constraint(edge_col, pltpu.HBM))


def finish_kernel(part_ref, proj_ref, out_ref):
    for sector in range(proj_ref.shape[0]):
        total = jnp.sum(part_ref[:, sector].astype(F32), axis=0).astype(BF16)
        out_ref[sector] = jnp.dot(total, proj_ref[sector], preferred_element_type=F32).astype(BF16)


def finish(parts, proj_col):
    _, sectors, piece, _ = parts.shape
    return pl.pallas_call(
        finish_kernel,
        out_shape=jax.ShapeDtypeStruct((sectors, piece, SIZE), BF16),
        in_specs=[VMEM] * 2,
        compiler_params=SMALL,
        name="finish",
    )(parts, proj_col)


def body(corner, edge_row, source_row, proj_row, edge_col, source_col, proj_col):
    lefts, rights = lax.axis_size("left"), lax.axis_size("right")
    left, right = lax.axis_index("left"), lax.axis_index("right")

    parity = [list(range(start, lefts, 2)) for start in range(2)]
    own = lax.all_to_all(
        jnp.broadcast_to(corner, (lefts // 2, SIZE, SIZE)), "left", 0, 0, axis_index_groups=parity, tiled=True
    )
    other = lax.ppermute(own, "left", [(i, i ^ 1) for i in range(lefts)])
    held = jnp.concatenate([own, other], axis=0)
    source = source_row // rights
    slots = source // 2 + jnp.where(source % 2 == left % 2, 0, lefts // 2)

    offsets = [p * FLIPS[0] ^ q * FLIPS[1] ^ z * FLIPS[2] for p in range(2) for q in range(2) for z in range(2)]
    peers = jnp.bitwise_xor(right, jnp.array(offsets[::-1], jnp.int32))
    outs = row_partial(slots, peers, held, edge_row)
    for phase in range(2):
        came = [flip(outs[2 * part], ORDERS[part][phase], rights) for part in range(3)]
        outs = halve(outs[1::2], came) if phase == 0 else meet(outs[1::2], came)
    came = [flip(outs[part], ORDERS[part][2], rights) for part in range(3)]
    absorbed, *parts = absorb(jnp.reshape(right, (1,)).astype(jnp.int32), outs, came, proj_row)

    for phase in range(1, 3):
        came = [flip(parts[part], ORDERS[part][2 - phase], rights) for part in range(3)]
        if phase < 2:
            parts = double(parts, came)
    pieces = [value for pair in zip(parts, came) for value in pair]

    inner = source_col - left * (rights * COUNT)
    offset = jnp.bitwise_xor(inner // COUNT, right)
    z = offset // 4
    q = offset // 2 % 2
    p = (offset + q) % 2
    partial_cols = col_partial((p * 4 + q * 2 + z) * COUNT + inner % COUNT, pieces, edge_col, lefts)
    col_parts = lax.all_to_all(partial_cols, "left", 0, 0, tiled=True)
    return absorbed, finish(col_parts, proj_col)


def solution(mesh):
    in_specs = (
        P(("left", "right"), None, None),
        P("left", "right", None, None),
        P("left", "right"),
        P("left", None, None),
        P("right", "left", None, None),
        P("right", "left"),
        P("right", None, None),
    )
    out_specs = (P(("left", "right"), None, None), P("right", "left", None))
    return jax.shard_map(body, mesh=mesh, in_specs=in_specs, out_specs=out_specs, check_vma=False)
```

```python
import functools

import jax
import jax.numpy as jnp
from jax import lax
from jax.experimental import pallas as pl
from jax.experimental.pallas import tpu as pltpu
from jax.sharding import PartitionSpec as P

F32 = jnp.float32
BF16 = jnp.bfloat16
SIZE = 256
COUNT = 2
FLAT = COUNT * SIZE
DEPTH = 4
FLIPS = (1, 3, 4)
ORDERS = ((0, 1, 2), (1, 2, 0), (2, 0, 1))
CUTS = (0, 208, 384, FLAT)
LENGTHS = tuple(CUTS[i + 1] - CUTS[i] for i in range(3))
VMEM = pl.BlockSpec(memory_space=pltpu.VMEM)
SMALL = pltpu.CompilerParams(vmem_limit_bytes=8 * 2**20)


def flip(value, pairing, size):
    return lax.ppermute(value, "right", [(i, i ^ FLIPS[pairing]) for i in range(size)])


def place_of(place, order):
    bits = [place // 4, place // 2 % 2, place % 2]
    return bits[order[0]] * 4 + bits[order[1]] * 2 + bits[order[2]]


def cost(flops, elements):
    return pl.CostEstimate(flops=flops, bytes_accessed=2 * elements, transcendentals=0)


def row_kernel(slot_ref, peer_ref, held_ref, edge_hbm, *refs):
    *out_refs, ring, sems = refs
    step, steps, depth = pl.program_id(0), pl.num_programs(0), ring.shape[0]
    place = steps - 1 - step
    first = peer_ref[step] * COUNT

    def fetch(later):
        slot = later % depth
        return [
            pltpu.make_async_copy(edge_hbm.at[peer_ref[later] * COUNT + i], ring.at[slot, i], sems.at[slot, i])
            for i in range(COUNT)
        ]

    @pl.when(step == 0)
    def _():
        for later in range(depth - 1):
            for copy in fetch(later):
                copy.start()

    @pl.when(step + depth - 1 < steps)
    def _():
        for copy in fetch(step + depth - 1):
            copy.start()

    for copy in fetch(step):
        copy.wait()
    edge_ref = ring.at[step % depth]
    values = []
    for sector in range(COUNT):
        total = jnp.dot(held_ref[slot_ref[first + sector, 0]], edge_ref[sector, 0], preferred_element_type=F32)
        for entry in range(1, edge_ref.shape[1]):
            total += jnp.dot(
                held_ref[slot_ref[first + sector, entry]], edge_ref[sector, entry], preferred_element_type=F32
            )
        values.append(total.T)
    flat = jnp.concatenate(values, axis=0)
    for part, order in enumerate(ORDERS):
        index = place_of(place, order)
        send_ref, keep_ref = out_refs[2 * part], out_refs[2 * part + 1]
        value = flat[CUTS[part] : CUTS[part + 1]]

        @pl.when(index >= 4)
        def _():
            send_ref[index - 4] = value.astype(BF16)

        @pl.when(index < 4)
        def _():
            keep_ref[index] = value


def row_partial(slots, peers, held, edge_row):
    entries = edge_row.shape[1]
    steps = peers.shape[0]
    outs = []
    for length in LENGTHS:
        outs.append(jax.ShapeDtypeStruct((steps // 2, length, SIZE), BF16))
        outs.append(jax.ShapeDtypeStruct((steps // 2, length, SIZE), F32))
    return pl.pallas_call(
        row_kernel,
        out_shape=tuple(outs),
        grid_spec=pltpu.PrefetchScalarGridSpec(
            num_scalar_prefetch=2,
            grid=(steps,),
            in_specs=[VMEM, pl.BlockSpec(memory_space=pl.ANY)],
            out_specs=tuple(VMEM for _ in outs),
            scratch_shapes=[
                pltpu.VMEM((DEPTH, COUNT, entries, SIZE, SIZE), BF16),
                pltpu.SemaphoreType.DMA((DEPTH, COUNT)),
            ],
        ),
        compiler_params=pltpu.CompilerParams(vmem_limit_bytes=24 * 2**20),
        cost_estimate=cost(2 * steps * COUNT * entries * SIZE**3, steps * COUNT * entries * SIZE**2),
        name="row_partial",
    )(slots, peers, held, pltpu.with_memory_space_constraint(edge_row, pltpu.HBM))


def meet_kernel(turn, *refs):
    for part in range(3):
        keep_ref, came_ref, out_ref = refs[2 * part], refs[2 * part + 1], refs[6 + part]
        for place in range(4):
            out_ref[place] = (keep_ref[place].astype(F32) + came_ref[place ^ turn].astype(F32)).astype(BF16)


def meet(keeps, came, turn):
    args = [value for pair in zip(keeps, came) for value in pair]
    return pl.pallas_call(
        functools.partial(meet_kernel, turn),
        out_shape=tuple(jax.ShapeDtypeStruct(value.shape, BF16) for value in keeps),
        in_specs=[VMEM] * 6,
        out_specs=tuple(VMEM for _ in range(3)),
        compiler_params=SMALL,
        cost_estimate=cost(4 * FLAT * SIZE, 16 * FLAT * SIZE),
        name="meet",
    )(*args)


def absorb_kernel(index_ref, proj_ref, *refs):
    ours_refs, came_refs, out_ref, part_refs = refs[:3], refs[3:6], refs[6], refs[7:]
    mine = []
    for part, order in enumerate(ORDERS):
        low, high = CUTS[part], CUTS[part + 1]
        for place in range(4):
            offset = place // 2 * FLIPS[order[1]] ^ place % 2 * FLIPS[order[2]]
            first = (index_ref[0] ^ offset) * COUNT
            total = (ours_refs[part][place].astype(F32) + came_refs[part][place ^ 1].astype(F32)).astype(BF16)
            pieces = []
            for sector in range(COUNT):
                start, stop = max(low, sector * SIZE), min(high, (sector + 1) * SIZE)
                if start < stop:
                    pieces.append(
                        jnp.dot(total[start - low : stop - low], proj_ref[first + sector], preferred_element_type=F32)
                    )
            value = jnp.concatenate(pieces, axis=0).astype(BF16)
            part_refs[part][place] = value
            if place == 0:
                mine.append(value)
    flat = jnp.concatenate(mine, axis=0)
    for sector in range(COUNT):
        out_ref[sector] = flat[sector * SIZE : (sector + 1) * SIZE].T


def absorb(index, ours, came, proj_row):
    outs = [jax.ShapeDtypeStruct((COUNT, SIZE, SIZE), BF16)]
    outs += [jax.ShapeDtypeStruct((4, length, SIZE), BF16) for length in LENGTHS]
    return pl.pallas_call(
        absorb_kernel,
        out_shape=tuple(outs),
        in_specs=[pl.BlockSpec(memory_space=pltpu.SMEM)] + [VMEM] * 7,
        out_specs=tuple(VMEM for _ in outs),
        compiler_params=SMALL,
        cost_estimate=cost(8 * COUNT * SIZE**3, 20 * FLAT * SIZE),
        name="absorb",
    )(index, proj_row, *ours, *came)


def col_kernel(slot_ref, *refs):
    piece_refs, (edge_hbm, out_ref, held, edge_ref, edge_sems) = refs[:6], refs[6:]
    step = pl.program_id(0)

    def fetch(later):
        return pltpu.make_async_copy(edge_hbm.at[later], edge_ref.at[later], edge_sems.at[later])

    @pl.when(step == 0)
    def _():
        for later in range(edge_ref.shape[0]):
            fetch(later).start()
        for part, order in enumerate(ORDERS):
            for place in range(8):
                index = place_of(place, order)
                start = place * FLAT + CUTS[part]
                held[start : start + LENGTHS[part]] = piece_refs[2 * part + index // 4][index % 4]

    fetch(step).wait()

    def block(entry):
        return held[pl.ds(pl.multiple_of(slot_ref[step, entry] * SIZE, SIZE), SIZE)]

    def term(entry):
        return lax.dot_general(
            edge_ref[step, entry], block(entry), (((1,), (1,)), ((), ())), preferred_element_type=F32
        )

    total = term(0)
    for entry in range(1, edge_ref.shape[1]):
        total += term(entry)
    out_ref[:, 0] = total.astype(BF16).reshape(out_ref.shape[0], out_ref.shape[2], SIZE)


def col_partial(slots, pieces_in, edge_col, pieces):
    sectors, entries = edge_col.shape[:2]
    piece = SIZE // pieces
    return pl.pallas_call(
        col_kernel,
        out_shape=jax.ShapeDtypeStruct((pieces, sectors, piece, SIZE), BF16),
        grid_spec=pltpu.PrefetchScalarGridSpec(
            num_scalar_prefetch=1,
            grid=(sectors,),
            in_specs=[VMEM] * 6 + [pl.BlockSpec(memory_space=pl.ANY)],
            out_specs=pl.BlockSpec((pieces, 1, piece, SIZE), lambda g, s: (0, g, 0, 0)),
            scratch_shapes=[
                pltpu.VMEM((8 * FLAT, SIZE), BF16),
                pltpu.VMEM(edge_col.shape, BF16),
                pltpu.SemaphoreType.DMA((sectors,)),
            ],
        ),
        compiler_params=pltpu.CompilerParams(vmem_limit_bytes=24 * 2**20),
        cost_estimate=cost(2 * sectors * entries * SIZE**3, sectors * entries * SIZE**2),
        name="col_partial",
    )(slots, *pieces_in, pltpu.with_memory_space_constraint(edge_col, pltpu.HBM))


def finish_kernel(part_ref, proj_ref, out_ref):
    for sector in range(proj_ref.shape[0]):
        total = jnp.sum(part_ref[:, sector].astype(F32), axis=0).astype(BF16)
        out_ref[sector] = jnp.dot(total, proj_ref[sector], preferred_element_type=F32).astype(BF16)


def finish(parts, proj_col):
    _, sectors, piece, _ = parts.shape
    return pl.pallas_call(
        finish_kernel,
        out_shape=jax.ShapeDtypeStruct((sectors, piece, SIZE), BF16),
        in_specs=[VMEM] * 2,
        compiler_params=SMALL,
        name="finish",
    )(parts, proj_col)


def body(corner, edge_row, source_row, proj_row, edge_col, source_col, proj_col):
    lefts, rights = lax.axis_size("left"), lax.axis_size("right")
    left, right = lax.axis_index("left"), lax.axis_index("right")

    parity = [list(range(start, lefts, 2)) for start in range(2)]
    own = lax.all_to_all(
        jnp.broadcast_to(corner, (lefts // 2, SIZE, SIZE)), "left", 0, 0, axis_index_groups=parity, tiled=True
    )
    other = lax.ppermute(own, "left", [(i, i ^ 1) for i in range(lefts)])
    held = jnp.concatenate([own, other], axis=0)
    source = source_row // rights
    slots = source // 2 + jnp.where(source % 2 == left % 2, 0, lefts // 2)

    offsets = [p * FLIPS[0] ^ q * FLIPS[1] ^ z * FLIPS[2] for p in range(2) for q in range(2) for z in range(2)]
    peers = jnp.bitwise_xor(right, jnp.array(offsets[::-1], jnp.int32))
    outs = row_partial(slots, peers, held, edge_row)
    came = [flip(outs[2 * part], ORDERS[part][0], rights) for part in range(3)]
    ours = meet(outs[1::2], came, 0)
    came = [flip(ours[part], ORDERS[part][1], rights) for part in range(3)]
    ours = meet(ours, came, 2)
    came = [flip(ours[part], ORDERS[part][2], rights) for part in range(3)]
    absorbed, *parts = absorb(jnp.reshape(right, (1,)).astype(jnp.int32), ours, came, proj_row)
    came = [flip(parts[part], ORDERS[part][0], rights) for part in range(3)]
    pieces = [value for pair in zip(parts, came) for value in pair]

    inner = source_col - left * (rights * COUNT)
    offset = jnp.bitwise_xor(inner // COUNT, right)
    z = offset // 4
    q = offset // 2 % 2
    p = (offset + q) % 2
    partial_cols = col_partial((p * 4 + q * 2 + z) * COUNT + inner % COUNT, pieces, edge_col, lefts)
    col_parts = lax.all_to_all(partial_cols, "left", 0, 0, tiled=True)
    return absorbed, finish(col_parts, proj_col)


def solution(mesh):
    in_specs = (
        P(("left", "right"), None, None),
        P("left", "right", None, None),
        P("left", "right"),
        P("left", None, None),
        P("right", "left", None, None),
        P("right", "left"),
        P("right", None, None),
    )
    out_specs = (P(("left", "right"), None, None), P("right", "left", None))
    return jax.shard_map(body, mesh=mesh, in_specs=in_specs, out_specs=out_specs, check_vma=False)
```

```python
import functools

import jax
import jax.numpy as jnp
from jax import lax
from jax.experimental import pallas as pl
from jax.experimental.pallas import tpu as pltpu
from jax.sharding import PartitionSpec as P

F32 = jnp.float32
BF16 = jnp.bfloat16
SIZE = 256
COUNT = 2
FLAT = COUNT * SIZE
HOPS = ((2, 1), (1, 1), (3, 1), (0, 1), (1, 0), (3, 0), (2, 0))
DEPTH = 4
FLIPS = (1, 3, 4)
ORDERS = ((0, 1, 2), (1, 2, 0), (2, 0, 1))
CUTS = (0, 208, 384, FLAT)
LENGTHS = tuple(CUTS[i + 1] - CUTS[i] for i in range(3))
VMEM = pl.BlockSpec(memory_space=pltpu.VMEM)
SMALL = pltpu.CompilerParams(vmem_limit_bytes=8 * 2**20)


def flip(value, pairing, size):
    return lax.ppermute(value, "right", [(i, i ^ FLIPS[pairing]) for i in range(size)])


def place_of(place, order):
    bits = [place // 4, place // 2 % 2, place % 2]
    return bits[order[0]] * 4 + bits[order[1]] * 2 + bits[order[2]]


def cost(flops, elements):
    return pl.CostEstimate(flops=flops, bytes_accessed=2 * elements, transcendentals=0)


def join_kernel(*refs):
    *block_refs, out_ref = refs
    for place, block_ref in enumerate(block_refs):
        out_ref[place] = block_ref[0]


def join(blocks):
    return pl.pallas_call(
        join_kernel,
        out_shape=jax.ShapeDtypeStruct((len(blocks), SIZE, SIZE), BF16),
        in_specs=[VMEM for _ in blocks],
        out_specs=VMEM,
        compiler_params=SMALL,
        cost_estimate=cost(0, 2 * len(blocks) * SIZE**2),
        name="join",
    )(*blocks)


def load_kernel(edge_ref, out_ref, sems):
    copies = [
        pltpu.make_async_copy(edge_ref.at[i], out_ref.at[i], sems.at[i]) for i in range(edge_ref.shape[0])
    ]
    for copy in copies:
        copy.start()
    for copy in copies:
        copy.wait()


def load(edge):
    return pl.pallas_call(
        load_kernel,
        out_shape=pltpu.VMEM(edge.shape, edge.dtype),
        in_specs=[pl.BlockSpec(memory_space=pl.ANY)],
        out_specs=VMEM,
        scratch_shapes=[pltpu.SemaphoreType.DMA((edge.shape[0],))],
        compiler_params=SMALL,
        cost_estimate=cost(0, 2 * edge.size),
        name="load",
    )(pltpu.with_memory_space_constraint(edge, pltpu.HBM))


def row_kernel(slot_ref, peer_ref, held_ref, edge_ref, *out_refs):
    step = pl.program_id(0)
    place = pl.num_programs(0) - 1 - step
    first = peer_ref[step] * COUNT

    values = []
    for sector in range(COUNT):
        total = jnp.dot(held_ref[slot_ref[0, first + sector]], edge_ref[first + sector, 0], preferred_element_type=F32)
        for entry in range(1, edge_ref.shape[1]):
            total += jnp.dot(
                held_ref[slot_ref[entry, first + sector]], edge_ref[first + sector, entry], preferred_element_type=F32
            )
        values.append(total.T)
    flat = jnp.concatenate(values, axis=0)
    for part, order in enumerate(ORDERS):
        index = place_of(place, order)
        send_ref, keep_ref = out_refs[2 * part], out_refs[2 * part + 1]
        value = flat[CUTS[part] : CUTS[part + 1]]

        @pl.when(index >= 4)
        def _():
            send_ref[index - 4] = value.astype(BF16)

        @pl.when(index < 4)
        def _():
            keep_ref[index] = value


def row_partial(slots, peers, held, edge_row):
    entries = edge_row.shape[1]
    steps = peers.shape[0]
    outs = []
    for length in LENGTHS:
        outs.append(jax.ShapeDtypeStruct((steps // 2, length, SIZE), BF16))
        outs.append(jax.ShapeDtypeStruct((steps // 2, length, SIZE), F32))
    return pl.pallas_call(
        row_kernel,
        out_shape=tuple(outs),
        grid_spec=pltpu.PrefetchScalarGridSpec(
            num_scalar_prefetch=2,
            grid=(steps,),
            in_specs=[VMEM, VMEM],
            out_specs=tuple(VMEM for _ in outs),
        ),
        compiler_params=SMALL,
        cost_estimate=cost(2 * steps * COUNT * entries * SIZE**3, steps * COUNT * entries * SIZE**2),
        name="row_partial",
    )(slots, peers, held, edge_row)


def meet_kernel(turn, *refs):
    for part in range(3):
        keep_ref, came_ref, out_ref = refs[2 * part], refs[2 * part + 1], refs[6 + part]
        for place in range(4):
            out_ref[place] = (keep_ref[place].astype(F32) + came_ref[place ^ turn].astype(F32)).astype(BF16)


def meet(keeps, came, turn):
    args = [value for pair in zip(keeps, came) for value in pair]
    return pl.pallas_call(
        functools.partial(meet_kernel, turn),
        out_shape=tuple(jax.ShapeDtypeStruct(value.shape, BF16) for value in keeps),
        in_specs=[VMEM] * 6,
        out_specs=tuple(VMEM for _ in range(3)),
        compiler_params=SMALL,
        cost_estimate=cost(4 * FLAT * SIZE, 16 * FLAT * SIZE),
        name="meet",
    )(*args)


def absorb_kernel(index_ref, proj_ref, *refs):
    ours_refs, came_refs, out_ref, part_refs = refs[:3], refs[3:6], refs[6], refs[7:]
    mine = []
    for part, order in enumerate(ORDERS):
        low, high = CUTS[part], CUTS[part + 1]
        for place in range(4):
            offset = place // 2 * FLIPS[order[1]] ^ place % 2 * FLIPS[order[2]]
            first = (index_ref[0] ^ offset) * COUNT
            total = (ours_refs[part][place].astype(F32) + came_refs[part][place ^ 1].astype(F32)).astype(BF16)
            pieces = []
            for sector in range(COUNT):
                start, stop = max(low, sector * SIZE), min(high, (sector + 1) * SIZE)
                if start < stop:
                    pieces.append(
                        jnp.dot(total[start - low : stop - low], proj_ref[first + sector], preferred_element_type=F32)
                    )
            value = jnp.concatenate(pieces, axis=0).astype(BF16)
            part_refs[part][place] = value
            if place == 0:
                mine.append(value)
    flat = jnp.concatenate(mine, axis=0)
    for sector in range(COUNT):
        out_ref[sector] = flat[sector * SIZE : (sector + 1) * SIZE].T


def absorb(index, ours, came, proj_row):
    outs = [jax.ShapeDtypeStruct((COUNT, SIZE, SIZE), BF16)]
    outs += [jax.ShapeDtypeStruct((4, length, SIZE), BF16) for length in LENGTHS]
    return pl.pallas_call(
        absorb_kernel,
        out_shape=tuple(outs),
        in_specs=[pl.BlockSpec(memory_space=pltpu.SMEM)] + [VMEM] * 7,
        out_specs=tuple(VMEM for _ in outs),
        compiler_params=SMALL,
        cost_estimate=cost(8 * COUNT * SIZE**3, 20 * FLAT * SIZE),
        name="absorb",
    )(index, proj_row, *ours, *came)


def col_kernel(slot_ref, *refs):
    piece_refs, (edge_ref, out_ref, held) = refs[:6], refs[6:]
    step = pl.program_id(0)

    @pl.when(step == 0)
    def _():
        for part, order in enumerate(ORDERS):
            for place in range(8):
                index = place_of(place, order)
                start = place * FLAT + CUTS[part]
                held[start : start + LENGTHS[part]] = piece_refs[2 * part + index // 4][index % 4]

    def block(entry):
        return held[pl.ds(pl.multiple_of(slot_ref[step, entry] * SIZE, SIZE), SIZE)]

    def term(entry):
        return lax.dot_general(
            edge_ref[step, entry], block(entry), (((1,), (1,)), ((), ())), preferred_element_type=F32
        )

    total = term(0)
    for entry in range(1, edge_ref.shape[1]):
        total += term(entry)
    out_ref[:, 0] = total.astype(BF16).reshape(out_ref.shape[0], out_ref.shape[2], SIZE)


def col_partial(slots, pieces_in, edge_col, pieces):
    sectors, entries = edge_col.shape[:2]
    piece = SIZE // pieces
    return pl.pallas_call(
        col_kernel,
        out_shape=jax.ShapeDtypeStruct((pieces, sectors, piece, SIZE), BF16),
        grid_spec=pltpu.PrefetchScalarGridSpec(
            num_scalar_prefetch=1,
            grid=(sectors,),
            in_specs=[VMEM] * 7,
            out_specs=pl.BlockSpec((pieces, 1, piece, SIZE), lambda g, s: (0, g, 0, 0)),
            scratch_shapes=[pltpu.VMEM((8 * FLAT, SIZE), BF16)],
        ),
        compiler_params=SMALL,
        cost_estimate=cost(2 * sectors * entries * SIZE**3, sectors * entries * SIZE**2),
        name="col_partial",
    )(slots, *pieces_in, edge_col)


def finish_kernel(part_ref, proj_ref, out_ref):
    for sector in range(proj_ref.shape[0]):
        total = jnp.sum(part_ref[:, sector].astype(F32), axis=0).astype(BF16)
        out_ref[sector] = jnp.dot(total, proj_ref[sector], preferred_element_type=F32).astype(BF16)


def finish(parts, proj_col):
    _, sectors, piece, _ = parts.shape
    return pl.pallas_call(
        finish_kernel,
        out_shape=jax.ShapeDtypeStruct((sectors, piece, SIZE), BF16),
        in_specs=[VMEM] * 2,
        compiler_params=SMALL,
        name="finish",
    )(parts, proj_col)


def body(corner, edge_row, source_row, proj_row, edge_col, source_col, proj_col):
    lefts, rights = lax.axis_size("left"), lax.axis_size("right")
    left, right = lax.axis_index("left"), lax.axis_index("right")
    rings, chips = lefts // 4, lefts // 2

    source = source_row.T // rights
    turn = (left // 4 - source // 4) % rings
    swap = (left // 2 + source // 2) % 2
    slots = swap * rings + turn + jnp.where(source % 2 == left % 2, 0, chips)
    offsets = [p * FLIPS[0] ^ q * FLIPS[1] ^ z * FLIPS[2] for p in range(2) for q in range(2) for z in range(2)]
    peers = jnp.bitwise_xor(right, jnp.array(offsets[::-1], jnp.int32))
    mine = jnp.reshape(right, (1,)).astype(jnp.int32)
    inner = source_col - left * (rights * COUNT)
    offset = jnp.bitwise_xor(inner // COUNT, right)
    z = offset // 4
    q = offset // 2 % 2
    p = (offset + q) % 2
    col_slots = (p * 4 + q * 2 + z) * COUNT + inner % COUNT

    def bring(turn, swap):
        pairs = []
        for ring in range(rings):
            for low in range(4):
                pairs.append((ring * 4 + low, (ring + turn) % rings * 4 + (low ^ (2 * swap))))
        return lax.ppermute(corner, "left", pairs)

    came = {hop: bring(*hop) for hop in HOPS}
    edge_row, slots, peers, mine, col_slots = lax.optimization_barrier((edge_row, slots, peers, mine, col_slots))
    edge_row = load(edge_row)
    came[HOPS[-1]], edge_row = lax.optimization_barrier((came[HOPS[-1]], edge_row))
    own = join([came[place % rings, place // rings] if place else corner for place in range(chips)])
    other = lax.ppermute(own, "left", [(i, i ^ 1) for i in range(lefts)])
    held = jnp.concatenate([own, other], axis=0)

    outs = row_partial(slots, peers, held, edge_row)
    came = [flip(outs[2 * part], ORDERS[part][0], rights) for part in range(3)]
    ours = meet(outs[1::2], came, 0)
    came = [flip(ours[part], ORDERS[part][1], rights) for part in range(3)]
    ours = meet(ours, came, 2)
    came = [flip(ours[part], ORDERS[part][2], rights) for part in range(3)]
    absorbed, *parts = absorb(mine, ours, came, proj_row)

    came = [flip(parts[part], ORDERS[part][0], rights) for part in range(3)]
    edge_col = load(edge_col)
    pieces = [value for pair in zip(parts, came) for value in pair]
    partial_cols = col_partial(col_slots, pieces, edge_col, lefts)
    col_parts = lax.all_to_all(partial_cols, "left", 0, 0, tiled=True)
    return absorbed, finish(col_parts, proj_col)


def solution(mesh):
    in_specs = (
        P(("left", "right"), None, None),
        P("left", "right", None, None),
        P("left", "right"),
        P("left", None, None),
        P("right", "left", None, None),
        P("right", "left"),
        P("right", None, None),
    )
    out_specs = (P(("left", "right"), None, None), P("right", "left", None))
    return jax.shard_map(body, mesh=mesh, in_specs=in_specs, out_specs=out_specs, check_vma=False)
```

```python
import functools

import jax
import jax.numpy as jnp
from jax import lax
from jax.experimental import pallas as pl
from jax.experimental.pallas import tpu as pltpu
from jax.sharding import PartitionSpec as P

F32 = jnp.float32
BF16 = jnp.bfloat16
SIZE = 256
COUNT = 2
FLAT = COUNT * SIZE
HOPS = ((2, 1), (1, 1), (3, 1), (0, 1), (2, 0), (1, 0), (3, 0))
DEPTH = 4
FLIPS = (1, 3, 4)
ORDERS = ((0, 1, 2), (1, 2, 0), (2, 0, 1))
CUTS = (0, 208, 384, FLAT)
LENGTHS = tuple(CUTS[i + 1] - CUTS[i] for i in range(3))
VMEM = pl.BlockSpec(memory_space=pltpu.VMEM)
SMALL = pltpu.CompilerParams(vmem_limit_bytes=8 * 2**20)


def flip(value, pairing, size):
    return lax.ppermute(value, "right", [(i, i ^ FLIPS[pairing]) for i in range(size)])


def place_of(place, order):
    bits = [place // 4, place // 2 % 2, place % 2]
    return bits[order[0]] * 4 + bits[order[1]] * 2 + bits[order[2]]


def cost(flops, elements):
    return pl.CostEstimate(flops=flops, bytes_accessed=2 * elements, transcendentals=0)


def join_kernel(*refs):
    *block_refs, out_ref = refs
    for place, block_ref in enumerate(block_refs):
        out_ref[place] = block_ref[0]


def join(blocks):
    return pl.pallas_call(
        join_kernel,
        out_shape=jax.ShapeDtypeStruct((len(blocks), SIZE, SIZE), BF16),
        in_specs=[VMEM for _ in blocks],
        out_specs=VMEM,
        compiler_params=SMALL,
        cost_estimate=cost(0, 2 * len(blocks) * SIZE**2),
        name="join",
    )(*blocks)


def load_kernel(edge_ref, out_ref, sems):
    copies = [
        pltpu.make_async_copy(edge_ref.at[i], out_ref.at[i], sems.at[i]) for i in range(edge_ref.shape[0])
    ]
    for copy in copies:
        copy.start()
    for copy in copies:
        copy.wait()


def load(edge):
    return pl.pallas_call(
        load_kernel,
        out_shape=pltpu.VMEM(edge.shape, edge.dtype),
        in_specs=[pl.BlockSpec(memory_space=pl.ANY)],
        out_specs=VMEM,
        scratch_shapes=[pltpu.SemaphoreType.DMA((edge.shape[0],))],
        compiler_params=SMALL,
        cost_estimate=cost(0, 2 * edge.size),
        name="load",
    )(pltpu.with_memory_space_constraint(edge, pltpu.HBM))


def row_kernel(source_ref, held_ref, edge_ref, *out_refs):
    rights, rings = lax.axis_size("right"), lax.axis_size("left") // 4
    left, right = lax.axis_index("left"), lax.axis_index("right")

    def slot(entry, sector):
        source = source_ref[entry, sector] // rights
        turn = (left // 4 - source // 4 + rings) % rings
        swap = (left // 2 + source // 2) % 2
        return ((source + left) % 2 * 2 + swap) * rings + turn

    def sums(place):
        offset = place // 4 * FLIPS[0] ^ place // 2 % 2 * FLIPS[1] ^ place % 2 * FLIPS[2]
        first = (right ^ offset) * COUNT
        values = []
        for sector in range(COUNT):
            here = first + sector
            total = jnp.dot(held_ref[slot(0, here)], edge_ref[here, 0], preferred_element_type=F32)
            for entry in range(1, edge_ref.shape[1]):
                total += jnp.dot(held_ref[slot(entry, here)], edge_ref[here, entry], preferred_element_type=F32)
            values.append(total.T)
        return jnp.concatenate(values, axis=0)

    step = pl.program_id(0)
    for last in range(2):
        place = (pl.num_programs(0) - 1 - step) * 2 + last
        flat = sums(place)
        for part, order in enumerate(ORDERS):
            index = place_of(place, order)
            send_ref, keep_ref = out_refs[2 * part], out_refs[2 * part + 1]
            value = flat[CUTS[part] : CUTS[part + 1]]
            if order[0] == 2:
                if last:
                    send_ref[index - 4] = value.astype(BF16)
                else:
                    keep_ref[index] = value
                continue

            @pl.when(index >= 4)
            def _():
                send_ref[index - 4] = value.astype(BF16)

            @pl.when(index < 4)
            def _():
                keep_ref[index] = value


def row_partial(source, held, edge_row):
    entries = edge_row.shape[1]
    steps = edge_row.shape[0] // (2 * COUNT)
    outs = []
    for length in LENGTHS:
        outs.append(jax.ShapeDtypeStruct((4, length, SIZE), BF16))
        outs.append(jax.ShapeDtypeStruct((4, length, SIZE), F32))
    return pl.pallas_call(
        row_kernel,
        out_shape=tuple(outs),
        grid_spec=pltpu.PrefetchScalarGridSpec(
            num_scalar_prefetch=1,
            grid=(steps,),
            in_specs=[VMEM, VMEM],
            out_specs=tuple(VMEM for _ in outs),
        ),
        compiler_params=SMALL,
        cost_estimate=cost(4 * steps * COUNT * entries * SIZE**3, steps * COUNT * entries * SIZE**2),
        name="row_partial",
    )(source, held, edge_row)


def meet_kernel(turn, *refs):
    for part in range(3):
        keep_ref, came_ref, out_ref = refs[2 * part], refs[2 * part + 1], refs[6 + part]
        for place in range(4):
            out_ref[place] = (keep_ref[place].astype(F32) + came_ref[place ^ turn].astype(F32)).astype(BF16)


def meet(keeps, came, turn):
    args = [value for pair in zip(keeps, came) for value in pair]
    return pl.pallas_call(
        functools.partial(meet_kernel, turn),
        out_shape=tuple(jax.ShapeDtypeStruct(value.shape, BF16) for value in keeps),
        in_specs=[VMEM] * 6,
        out_specs=tuple(VMEM for _ in range(3)),
        compiler_params=SMALL,
        cost_estimate=cost(4 * FLAT * SIZE, 16 * FLAT * SIZE),
        name="meet",
    )(*args)


def absorb_kernel(proj_ref, *refs):
    right = lax.axis_index("right")
    ours_refs, came_refs, out_ref, part_refs = refs[:3], refs[3:6], refs[6], refs[7:]
    mine = []
    for part, order in enumerate(ORDERS):
        low, high = CUTS[part], CUTS[part + 1]
        for place in range(4):
            offset = place // 2 * FLIPS[order[1]] ^ place % 2 * FLIPS[order[2]]
            first = (right ^ offset) * COUNT
            total = (ours_refs[part][place].astype(F32) + came_refs[part][place ^ 1].astype(F32)).astype(BF16)
            pieces = []
            for sector in range(COUNT):
                start, stop = max(low, sector * SIZE), min(high, (sector + 1) * SIZE)
                if start < stop:
                    pieces.append(
                        jnp.dot(total[start - low : stop - low], proj_ref[first + sector], preferred_element_type=F32)
                    )
            value = jnp.concatenate(pieces, axis=0).astype(BF16)
            part_refs[part][place] = value
            if place == 0:
                mine.append(value)
    flat = jnp.concatenate(mine, axis=0)
    for sector in range(COUNT):
        out_ref[sector] = flat[sector * SIZE : (sector + 1) * SIZE].T


def absorb(ours, came, proj_row):
    outs = [jax.ShapeDtypeStruct((COUNT, SIZE, SIZE), BF16)]
    outs += [jax.ShapeDtypeStruct((4, length, SIZE), BF16) for length in LENGTHS]
    return pl.pallas_call(
        absorb_kernel,
        out_shape=tuple(outs),
        in_specs=[VMEM] * 7,
        out_specs=tuple(VMEM for _ in outs),
        compiler_params=SMALL,
        cost_estimate=cost(8 * COUNT * SIZE**3, 20 * FLAT * SIZE),
        name="absorb",
    )(proj_row, *ours, *came)


def col_kernel(source_ref, *refs):
    piece_refs, (edge_ref, out_ref, held) = refs[:6], refs[6:]
    step = pl.program_id(0)

    @pl.when(step == 0)
    def _():
        for part, order in enumerate(ORDERS):
            for place in range(8):
                index = place_of(place, order)
                start = place * FLAT + CUTS[part]
                held[start : start + LENGTHS[part]] = piece_refs[2 * part + index // 4][index % 4]

    rights, left, right = lax.axis_size("right"), lax.axis_index("left"), lax.axis_index("right")

    def block(entry):
        inner = source_ref[step, entry] - left * (rights * COUNT)
        offset = inner // COUNT ^ right
        z = offset // 4
        q = offset // 2 % 2
        p = (offset + q) % 2
        slot = (p * 4 + q * 2 + z) * COUNT + inner % COUNT
        return held[pl.ds(pl.multiple_of(slot * SIZE, SIZE), SIZE)]

    def term(entry):
        return lax.dot_general(
            edge_ref[step, entry], block(entry), (((1,), (1,)), ((), ())), preferred_element_type=F32
        )

    total = term(0)
    for entry in range(1, edge_ref.shape[1]):
        total += term(entry)
    out_ref[:, 0] = total.astype(BF16).reshape(out_ref.shape[0], out_ref.shape[2], SIZE)


def col_partial(slots, pieces_in, edge_col, pieces):
    sectors, entries = edge_col.shape[:2]
    piece = SIZE // pieces
    return pl.pallas_call(
        col_kernel,
        out_shape=jax.ShapeDtypeStruct((pieces, sectors, piece, SIZE), BF16),
        grid_spec=pltpu.PrefetchScalarGridSpec(
            num_scalar_prefetch=1,
            grid=(sectors,),
            in_specs=[VMEM] * 7,
            out_specs=pl.BlockSpec((pieces, 1, piece, SIZE), lambda g, s: (0, g, 0, 0)),
            scratch_shapes=[pltpu.VMEM((8 * FLAT, SIZE), BF16)],
        ),
        compiler_params=SMALL,
        cost_estimate=cost(2 * sectors * entries * SIZE**3, sectors * entries * SIZE**2),
        name="col_partial",
    )(slots, *pieces_in, edge_col)


def finish_kernel(part_ref, proj_ref, out_ref):
    for sector in range(proj_ref.shape[0]):
        total = jnp.sum(part_ref[:, sector].astype(F32), axis=0).astype(BF16)
        out_ref[sector] = jnp.dot(total, proj_ref[sector], preferred_element_type=F32).astype(BF16)


def finish(parts, proj_col):
    _, sectors, piece, _ = parts.shape
    return pl.pallas_call(
        finish_kernel,
        out_shape=jax.ShapeDtypeStruct((sectors, piece, SIZE), BF16),
        in_specs=[VMEM] * 2,
        compiler_params=SMALL,
        name="finish",
    )(parts, proj_col)


def body(corner, edge_row, source_row, proj_row, edge_col, source_col, proj_col):
    lefts, rights = lax.axis_size("left"), lax.axis_size("right")
    rings = lefts // 4

    def bring(turn, swap):
        pairs = []
        for ring in range(rings):
            for low in range(4):
                pairs.append((ring * 4 + low, (ring + turn) % rings * 4 + (low ^ (2 * swap))))
        return lax.ppermute(corner, "left", pairs)

    came = {hop: bring(*hop) for hop in HOPS}
    edge_row = load(edge_row)
    came[HOPS[-1]], edge_row = lax.optimization_barrier((came[HOPS[-1]], edge_row))
    owns, others = [], []
    for far in (1, 0):
        blocks = [came[turn, far] if turn or far else corner for turn in range(rings)]
        owns.insert(0, join(blocks))
        others.insert(0, lax.ppermute(owns[0], "left", [(i, i ^ 1) for i in range(lefts)]))
    held = jnp.concatenate(owns + others, axis=0)

    outs = row_partial(source_row.T, held, edge_row)
    came = [flip(outs[2 * part], ORDERS[part][0], rights) for part in range(3)]
    ours = meet(outs[1::2], came, 0)
    came = [flip(ours[part], ORDERS[part][1], rights) for part in range(3)]
    ours = meet(ours, came, 2)
    came = [flip(ours[part], ORDERS[part][2], rights) for part in range(3)]
    absorbed, *parts = absorb(ours, came, proj_row)

    came = [flip(parts[part], ORDERS[part][0], rights) for part in range(3)]
    edge_col = load(edge_col)
    pieces = [value for pair in zip(parts, came) for value in pair]
    partial_cols = col_partial(source_col, pieces, edge_col, lefts)
    col_parts = lax.all_to_all(partial_cols, "left", 0, 0, tiled=True)
    return absorbed, finish(col_parts, proj_col)


def solution(mesh):
    in_specs = (
        P(("left", "right"), None, None),
        P("left", "right", None, None),
        P("left", "right"),
        P("left", None, None),
        P("right", "left", None, None),
        P("right", "left"),
        P("right", None, None),
    )
    out_specs = (P(("left", "right"), None, None), P("right", "left", None))
    return jax.shard_map(body, mesh=mesh, in_specs=in_specs, out_specs=out_specs, check_vma=False)
```

```python
import functools

import jax
import jax.numpy as jnp
from jax import lax
from jax.experimental import pallas as pl
from jax.experimental.pallas import tpu as pltpu
from jax.sharding import PartitionSpec as P

F32 = jnp.float32
BF16 = jnp.bfloat16
SIZE = 256
COUNT = 2
FLAT = COUNT * SIZE
HOPS = ((2, 1), (1, 1), (3, 1), (0, 1), (1, 0), (3, 0), (2, 0))
DEPTH = 4
FLIPS = (1, 3, 4)
ORDERS = ((0, 1, 2), (1, 2, 0), (2, 0, 1))
CUTS = (0, 208, 384, FLAT)
LENGTHS = tuple(CUTS[i + 1] - CUTS[i] for i in range(3))
VMEM = pl.BlockSpec(memory_space=pltpu.VMEM)
SMALL = pltpu.CompilerParams(vmem_limit_bytes=8 * 2**20)


def flip(value, pairing, size):
    return lax.ppermute(value, "right", [(i, i ^ FLIPS[pairing]) for i in range(size)])


def place_of(place, order):
    bits = [place // 4, place // 2 % 2, place % 2]
    return bits[order[0]] * 4 + bits[order[1]] * 2 + bits[order[2]]


def cost(flops, elements):
    return pl.CostEstimate(flops=flops, bytes_accessed=2 * elements, transcendentals=0)


def join_kernel(*refs):
    *block_refs, out_ref = refs
    for place, block_ref in enumerate(block_refs):
        out_ref[place] = block_ref[0]


def join(blocks):
    return pl.pallas_call(
        join_kernel,
        out_shape=jax.ShapeDtypeStruct((len(blocks), SIZE, SIZE), BF16),
        in_specs=[VMEM for _ in blocks],
        out_specs=VMEM,
        compiler_params=SMALL,
        cost_estimate=cost(0, 2 * len(blocks) * SIZE**2),
        name="join",
    )(*blocks)


def load_kernel(edge_ref, out_ref, sems):
    copies = [
        pltpu.make_async_copy(edge_ref.at[i], out_ref.at[i], sems.at[i]) for i in range(edge_ref.shape[0])
    ]
    for copy in copies:
        copy.start()
    for copy in copies:
        copy.wait()


def load(edge):
    return pl.pallas_call(
        load_kernel,
        out_shape=pltpu.VMEM(edge.shape, edge.dtype),
        in_specs=[pl.BlockSpec(memory_space=pl.ANY)],
        out_specs=VMEM,
        scratch_shapes=[pltpu.SemaphoreType.DMA((edge.shape[0],))],
        compiler_params=SMALL,
        cost_estimate=cost(0, 2 * edge.size),
        name="load",
    )(pltpu.with_memory_space_constraint(edge, pltpu.HBM))


def row_kernel(source_ref, held_ref, edge_ref, *out_refs):
    rights, rings = lax.axis_size("right"), lax.axis_size("left") // 4
    left, right = lax.axis_index("left"), lax.axis_index("right")

    def slot(entry, sector):
        source = source_ref[entry, sector] // rights
        turn = (left // 4 - source // 4 + rings) % rings
        swap = (left // 2 + source // 2) % 2
        return ((source + left) % 2 * 2 + swap) * rings + turn

    def sums(place):
        offset = place // 4 * FLIPS[0] ^ place // 2 % 2 * FLIPS[1] ^ place % 2 * FLIPS[2]
        first = (right ^ offset) * COUNT
        values = []
        for sector in range(COUNT):
            here = first + sector
            total = jnp.dot(held_ref[slot(0, here)], edge_ref[here, 0], preferred_element_type=F32)
            for entry in range(1, edge_ref.shape[1]):
                total += jnp.dot(held_ref[slot(entry, here)], edge_ref[here, entry], preferred_element_type=F32)
            values.append(total.T)
        return jnp.concatenate(values, axis=0)

    step = pl.program_id(0)
    for last in range(2):
        place = (pl.num_programs(0) - 1 - step) * 2 + last
        flat = sums(place)
        for part, order in enumerate(ORDERS):
            index = place_of(place, order)
            send_ref, keep_ref = out_refs[2 * part], out_refs[2 * part + 1]
            value = flat[CUTS[part] : CUTS[part + 1]]
            if order[0] == 2:
                if last:
                    send_ref[index - 4] = value.astype(BF16)
                else:
                    keep_ref[index] = value
                continue

            @pl.when(index >= 4)
            def _():
                send_ref[index - 4] = value.astype(BF16)

            @pl.when(index < 4)
            def _():
                keep_ref[index] = value


def row_partial(source, held, edge_row):
    entries = edge_row.shape[1]
    steps = edge_row.shape[0] // (2 * COUNT)
    outs = []
    for length in LENGTHS:
        outs.append(jax.ShapeDtypeStruct((4, length, SIZE), BF16))
        outs.append(jax.ShapeDtypeStruct((4, length, SIZE), F32))
    return pl.pallas_call(
        row_kernel,
        out_shape=tuple(outs),
        grid_spec=pltpu.PrefetchScalarGridSpec(
            num_scalar_prefetch=1,
            grid=(steps,),
            in_specs=[VMEM, VMEM],
            out_specs=tuple(VMEM for _ in outs),
        ),
        compiler_params=SMALL,
        cost_estimate=cost(4 * steps * COUNT * entries * SIZE**3, steps * COUNT * entries * SIZE**2),
        name="row_partial",
    )(source, held, edge_row)


def meet_kernel(turn, *refs):
    for part in range(3):
        keep_ref, came_ref, out_ref = refs[2 * part], refs[2 * part + 1], refs[6 + part]
        for place in range(4):
            out_ref[place] = (keep_ref[place].astype(F32) + came_ref[place ^ turn].astype(F32)).astype(BF16)


def meet(keeps, came, turn):
    args = [value for pair in zip(keeps, came) for value in pair]
    return pl.pallas_call(
        functools.partial(meet_kernel, turn),
        out_shape=tuple(jax.ShapeDtypeStruct(value.shape, BF16) for value in keeps),
        in_specs=[VMEM] * 6,
        out_specs=tuple(VMEM for _ in range(3)),
        compiler_params=SMALL,
        cost_estimate=cost(4 * FLAT * SIZE, 16 * FLAT * SIZE),
        name="meet",
    )(*args)


def absorb_kernel(proj_ref, *refs):
    right = lax.axis_index("right")
    ours_refs, came_refs, out_ref, part_refs = refs[:3], refs[3:6], refs[6], refs[7:]
    mine = []
    for part, order in enumerate(ORDERS):
        low, high = CUTS[part], CUTS[part + 1]
        for place in range(4):
            offset = place // 2 * FLIPS[order[1]] ^ place % 2 * FLIPS[order[2]]
            first = (right ^ offset) * COUNT
            total = (ours_refs[part][place].astype(F32) + came_refs[part][place ^ 1].astype(F32)).astype(BF16)
            pieces = []
            for sector in range(COUNT):
                start, stop = max(low, sector * SIZE), min(high, (sector + 1) * SIZE)
                if start < stop:
                    pieces.append(
                        jnp.dot(total[start - low : stop - low], proj_ref[first + sector], preferred_element_type=F32)
                    )
            value = jnp.concatenate(pieces, axis=0).astype(BF16)
            part_refs[part][place] = value
            if place == 0:
                mine.append(value)
    flat = jnp.concatenate(mine, axis=0)
    for sector in range(COUNT):
        out_ref[sector] = flat[sector * SIZE : (sector + 1) * SIZE].T


def absorb(ours, came, proj_row):
    outs = [jax.ShapeDtypeStruct((COUNT, SIZE, SIZE), BF16)]
    outs += [jax.ShapeDtypeStruct((4, length, SIZE), BF16) for length in LENGTHS]
    return pl.pallas_call(
        absorb_kernel,
        out_shape=tuple(outs),
        in_specs=[VMEM] * 7,
        out_specs=tuple(VMEM for _ in outs),
        compiler_params=SMALL,
        cost_estimate=cost(8 * COUNT * SIZE**3, 20 * FLAT * SIZE),
        name="absorb",
    )(proj_row, *ours, *came)


def col_kernel(source_ref, *refs):
    piece_refs, (edge_ref, out_ref, held) = refs[:6], refs[6:]
    step = pl.program_id(0)

    @pl.when(step == 0)
    def _():
        for part, order in enumerate(ORDERS):
            for place in range(8):
                index = place_of(place, order)
                start = place * FLAT + CUTS[part]
                held[start : start + LENGTHS[part]] = piece_refs[2 * part + index // 4][index % 4]

    rights, left, right = lax.axis_size("right"), lax.axis_index("left"), lax.axis_index("right")

    def block(entry):
        inner = source_ref[step, entry] - left * (rights * COUNT)
        offset = inner // COUNT ^ right
        z = offset // 4
        q = offset // 2 % 2
        p = (offset + q) % 2
        slot = (p * 4 + q * 2 + z) * COUNT + inner % COUNT
        return held[pl.ds(pl.multiple_of(slot * SIZE, SIZE), SIZE)]

    def term(entry):
        return lax.dot_general(
            edge_ref[step, entry], block(entry), (((1,), (1,)), ((), ())), preferred_element_type=F32
        )

    total = term(0)
    for entry in range(1, edge_ref.shape[1]):
        total += term(entry)
    out_ref[:, 0] = total.astype(BF16).reshape(out_ref.shape[0], out_ref.shape[2], SIZE)


def col_partial(slots, pieces_in, edge_col, pieces):
    sectors, entries = edge_col.shape[:2]
    piece = SIZE // pieces
    return pl.pallas_call(
        col_kernel,
        out_shape=jax.ShapeDtypeStruct((pieces, sectors, piece, SIZE), BF16),
        grid_spec=pltpu.PrefetchScalarGridSpec(
            num_scalar_prefetch=1,
            grid=(sectors,),
            in_specs=[VMEM] * 7,
            out_specs=pl.BlockSpec((pieces, 1, piece, SIZE), lambda g, s: (0, g, 0, 0)),
            scratch_shapes=[pltpu.VMEM((8 * FLAT, SIZE), BF16)],
        ),
        compiler_params=SMALL,
        cost_estimate=cost(2 * sectors * entries * SIZE**3, sectors * entries * SIZE**2),
        name="col_partial",
    )(slots, *pieces_in, edge_col)


def finish_kernel(part_ref, proj_ref, out_ref):
    for sector in range(proj_ref.shape[0]):
        total = jnp.sum(part_ref[:, sector].astype(F32), axis=0).astype(BF16)
        out_ref[sector] = jnp.dot(total, proj_ref[sector], preferred_element_type=F32).astype(BF16)


def finish(parts, proj_col):
    _, sectors, piece, _ = parts.shape
    return pl.pallas_call(
        finish_kernel,
        out_shape=jax.ShapeDtypeStruct((sectors, piece, SIZE), BF16),
        in_specs=[VMEM] * 2,
        compiler_params=SMALL,
        name="finish",
    )(parts, proj_col)


def body(corner, edge_row, source_row, proj_row, edge_col, source_col, proj_col):
    lefts, rights = lax.axis_size("left"), lax.axis_size("right")
    rings = lefts // 4

    def bring(turn, swap):
        pairs = []
        for ring in range(rings):
            for low in range(4):
                pairs.append((ring * 4 + low, (ring + turn) % rings * 4 + (low ^ (2 * swap))))
        return lax.ppermute(corner, "left", pairs)

    came = {hop: bring(*hop) for hop in HOPS}
    edge_row = load(edge_row)
    came[HOPS[-1]], edge_row = lax.optimization_barrier((came[HOPS[-1]], edge_row))
    owns, others = [], []
    for far in (1, 0):
        blocks = [came[turn, far] if turn or far else corner for turn in range(rings)]
        owns.insert(0, join(blocks))
        others.insert(0, lax.ppermute(owns[0], "left", [(i, i ^ 1) for i in range(lefts)]))
    held = jnp.concatenate(owns + others, axis=0)

    outs = row_partial(source_row.T, held, edge_row)
    came = [flip(outs[2 * part], ORDERS[part][0], rights) for part in range(3)]
    ours = meet(outs[1::2], came, 0)
    came = [flip(ours[part], ORDERS[part][1], rights) for part in range(3)]
    ours = meet(ours, came, 2)
    came = [flip(ours[part], ORDERS[part][2], rights) for part in range(3)]
    absorbed, *parts = absorb(ours, came, proj_row)

    came = [flip(parts[part], ORDERS[part][0], rights) for part in range(3)]
    edge_col = load(edge_col)
    pieces = [value for pair in zip(parts, came) for value in pair]
    partial_cols = col_partial(source_col, pieces, edge_col, lefts)
    col_parts = lax.all_to_all(partial_cols, "left", 0, 0, tiled=True)
    return absorbed, finish(col_parts, proj_col)


def solution(mesh):
    in_specs = (
        P(("left", "right"), None, None),
        P("left", "right", None, None),
        P("left", "right"),
        P("left", None, None),
        P("right", "left", None, None),
        P("right", "left"),
        P("right", None, None),
    )
    out_specs = (P(("left", "right"), None, None), P("right", "left", None))
    return jax.shard_map(body, mesh=mesh, in_specs=in_specs, out_specs=out_specs, check_vma=False)
```

```python
import functools

import jax
import jax.numpy as jnp
from jax import lax
from jax.experimental import pallas as pl
from jax.experimental.pallas import tpu as pltpu
from jax.sharding import PartitionSpec as P

F32 = jnp.float32
BF16 = jnp.bfloat16
SIZE = 256
COUNT = 2
FLAT = COUNT * SIZE
HOPS = ((2, 1), (3, 1), (1, 1), (0, 1), (3, 0), (1, 0), (2, 0))
DEPTH = 4
FLIPS = (1, 3, 4)
ORDERS = ((0, 1, 2), (1, 2, 0), (2, 0, 1))
CUTS = (0, 208, 384, FLAT)
LENGTHS = tuple(CUTS[i + 1] - CUTS[i] for i in range(3))
VMEM = pl.BlockSpec(memory_space=pltpu.VMEM)
SMALL = pltpu.CompilerParams(vmem_limit_bytes=8 * 2**20)


def flip(value, pairing, size):
    return lax.ppermute(value, "right", [(i, i ^ FLIPS[pairing]) for i in range(size)])


def place_of(place, order):
    bits = [place // 4, place // 2 % 2, place % 2]
    return bits[order[0]] * 4 + bits[order[1]] * 2 + bits[order[2]]


def cost(flops, elements):
    return pl.CostEstimate(flops=flops, bytes_accessed=2 * elements, transcendentals=0)


def join_kernel(*refs):
    *block_refs, out_ref = refs
    for place, block_ref in enumerate(block_refs):
        out_ref[place] = block_ref[0]


def join(blocks):
    return pl.pallas_call(
        join_kernel,
        out_shape=jax.ShapeDtypeStruct((len(blocks), SIZE, SIZE), BF16),
        in_specs=[VMEM for _ in blocks],
        out_specs=VMEM,
        compiler_params=SMALL,
        cost_estimate=cost(0, 2 * len(blocks) * SIZE**2),
        name="join",
    )(*blocks)


def load_kernel(edge_ref, out_ref, sems):
    copies = [
        pltpu.make_async_copy(edge_ref.at[i], out_ref.at[i], sems.at[i]) for i in range(edge_ref.shape[0])
    ]
    for copy in copies:
        copy.start()
    for copy in copies:
        copy.wait()


def load(edge):
    return pl.pallas_call(
        load_kernel,
        out_shape=pltpu.VMEM(edge.shape, edge.dtype),
        in_specs=[pl.BlockSpec(memory_space=pl.ANY)],
        out_specs=VMEM,
        scratch_shapes=[pltpu.SemaphoreType.DMA((edge.shape[0],))],
        compiler_params=SMALL,
        cost_estimate=cost(0, 2 * edge.size),
        name="load",
    )(pltpu.with_memory_space_constraint(edge, pltpu.HBM))


def row_kernel(source_ref, held_ref, edge_ref, *out_refs):
    rights, rings = lax.axis_size("right"), lax.axis_size("left") // 4
    left, right = lax.axis_index("left"), lax.axis_index("right")

    def slot(entry, sector):
        source = source_ref[entry, sector] // rights
        turn = (left // 4 - source // 4 + rings) % rings
        swap = (left // 2 + source // 2) % 2
        return ((source + left) % 2 * 2 + swap) * rings + turn

    def sums(place):
        offset = place // 4 * FLIPS[0] ^ place // 2 % 2 * FLIPS[1] ^ place % 2 * FLIPS[2]
        first = (right ^ offset) * COUNT
        values = []
        for sector in range(COUNT):
            here = first + sector
            total = jnp.dot(held_ref[slot(0, here)], edge_ref[here, 0], preferred_element_type=F32)
            for entry in range(1, edge_ref.shape[1]):
                total += jnp.dot(held_ref[slot(entry, here)], edge_ref[here, entry], preferred_element_type=F32)
            values.append(total.T)
        return jnp.concatenate(values, axis=0)

    step = pl.program_id(0)
    for last in range(2):
        place = (pl.num_programs(0) - 1 - step) * 2 + last
        flat = sums(place)
        for part, order in enumerate(ORDERS):
            index = place_of(place, order)
            send_ref, keep_ref = out_refs[2 * part], out_refs[2 * part + 1]
            value = flat[CUTS[part] : CUTS[part + 1]]
            if order[0] == 2:
                if last:
                    send_ref[index - 4] = value.astype(BF16)
                else:
                    keep_ref[index] = value
                continue

            @pl.when(index >= 4)
            def _():
                send_ref[index - 4] = value.astype(BF16)

            @pl.when(index < 4)
            def _():
                keep_ref[index] = value


def row_partial(source, held, edge_row):
    entries = edge_row.shape[1]
    steps = edge_row.shape[0] // (2 * COUNT)
    outs = []
    for length in LENGTHS:
        outs.append(jax.ShapeDtypeStruct((4, length, SIZE), BF16))
        outs.append(jax.ShapeDtypeStruct((4, length, SIZE), F32))
    return pl.pallas_call(
        row_kernel,
        out_shape=tuple(outs),
        grid_spec=pltpu.PrefetchScalarGridSpec(
            num_scalar_prefetch=1,
            grid=(steps,),
            in_specs=[VMEM, VMEM],
            out_specs=tuple(VMEM for _ in outs),
        ),
        compiler_params=SMALL,
        cost_estimate=cost(4 * steps * COUNT * entries * SIZE**3, steps * COUNT * entries * SIZE**2),
        name="row_partial",
    )(source, held, edge_row)


def meet_kernel(turn, *refs):
    for part in range(3):
        keep_ref, came_ref, out_ref = refs[2 * part], refs[2 * part + 1], refs[6 + part]
        for place in range(4):
            out_ref[place] = (keep_ref[place].astype(F32) + came_ref[place ^ turn].astype(F32)).astype(BF16)


def meet(keeps, came, turn):
    args = [value for pair in zip(keeps, came) for value in pair]
    return pl.pallas_call(
        functools.partial(meet_kernel, turn),
        out_shape=tuple(jax.ShapeDtypeStruct(value.shape, BF16) for value in keeps),
        in_specs=[VMEM] * 6,
        out_specs=tuple(VMEM for _ in range(3)),
        compiler_params=SMALL,
        cost_estimate=cost(4 * FLAT * SIZE, 16 * FLAT * SIZE),
        name="meet",
    )(*args)


def absorb_kernel(proj_ref, *refs):
    right = lax.axis_index("right")
    ours_refs, came_refs, out_ref, part_refs = refs[:3], refs[3:6], refs[6], refs[7:]
    mine = []
    for part, order in enumerate(ORDERS):
        low, high = CUTS[part], CUTS[part + 1]
        for place in range(4):
            offset = place // 2 * FLIPS[order[1]] ^ place % 2 * FLIPS[order[2]]
            first = (right ^ offset) * COUNT
            total = (ours_refs[part][place].astype(F32) + came_refs[part][place ^ 1].astype(F32)).astype(BF16)
            pieces = []
            for sector in range(COUNT):
                start, stop = max(low, sector * SIZE), min(high, (sector + 1) * SIZE)
                if start < stop:
                    pieces.append(
                        jnp.dot(total[start - low : stop - low], proj_ref[first + sector], preferred_element_type=F32)
                    )
            value = jnp.concatenate(pieces, axis=0).astype(BF16)
            part_refs[part][place] = value
            if place == 0:
                mine.append(value)
    flat = jnp.concatenate(mine, axis=0)
    for sector in range(COUNT):
        out_ref[sector] = flat[sector * SIZE : (sector + 1) * SIZE].T


def absorb(ours, came, proj_row):
    outs = [jax.ShapeDtypeStruct((COUNT, SIZE, SIZE), BF16)]
    outs += [jax.ShapeDtypeStruct((4, length, SIZE), BF16) for length in LENGTHS]
    return pl.pallas_call(
        absorb_kernel,
        out_shape=tuple(outs),
        in_specs=[VMEM] * 7,
        out_specs=tuple(VMEM for _ in outs),
        compiler_params=SMALL,
        cost_estimate=cost(8 * COUNT * SIZE**3, 20 * FLAT * SIZE),
        name="absorb",
    )(proj_row, *ours, *came)


def col_kernel(source_ref, *refs):
    piece_refs, (edge_ref, out_ref, held) = refs[:6], refs[6:]
    step = pl.program_id(0)

    @pl.when(step == 0)
    def _():
        for part, order in enumerate(ORDERS):
            for place in range(8):
                index = place_of(place, order)
                start = place * FLAT + CUTS[part]
                held[start : start + LENGTHS[part]] = piece_refs[2 * part + index // 4][index % 4]

    rights, left, right = lax.axis_size("right"), lax.axis_index("left"), lax.axis_index("right")

    def block(entry):
        inner = source_ref[step, entry] - left * (rights * COUNT)
        offset = inner // COUNT ^ right
        z = offset // 4
        q = offset // 2 % 2
        p = (offset + q) % 2
        slot = (p * 4 + q * 2 + z) * COUNT + inner % COUNT
        return held[pl.ds(pl.multiple_of(slot * SIZE, SIZE), SIZE)]

    def term(entry):
        return lax.dot_general(
            edge_ref[step, entry], block(entry), (((1,), (1,)), ((), ())), preferred_element_type=F32
        )

    total = term(0)
    for entry in range(1, edge_ref.shape[1]):
        total += term(entry)
    out_ref[:, 0] = total.astype(BF16).reshape(out_ref.shape[0], out_ref.shape[2], SIZE)


def col_partial(slots, pieces_in, edge_col, pieces):
    sectors, entries = edge_col.shape[:2]
    piece = SIZE // pieces
    return pl.pallas_call(
        col_kernel,
        out_shape=jax.ShapeDtypeStruct((pieces, sectors, piece, SIZE), BF16),
        grid_spec=pltpu.PrefetchScalarGridSpec(
            num_scalar_prefetch=1,
            grid=(sectors,),
            in_specs=[VMEM] * 7,
            out_specs=pl.BlockSpec((pieces, 1, piece, SIZE), lambda g, s: (0, g, 0, 0)),
            scratch_shapes=[pltpu.VMEM((8 * FLAT, SIZE), BF16)],
        ),
        compiler_params=SMALL,
        cost_estimate=cost(2 * sectors * entries * SIZE**3, sectors * entries * SIZE**2),
        name="col_partial",
    )(slots, *pieces_in, edge_col)


def finish_kernel(part_ref, proj_ref, out_ref):
    for sector in range(proj_ref.shape[0]):
        total = jnp.sum(part_ref[:, sector].astype(F32), axis=0).astype(BF16)
        out_ref[sector] = jnp.dot(total, proj_ref[sector], preferred_element_type=F32).astype(BF16)


def finish(parts, proj_col):
    _, sectors, piece, _ = parts.shape
    return pl.pallas_call(
        finish_kernel,
        out_shape=jax.ShapeDtypeStruct((sectors, piece, SIZE), BF16),
        in_specs=[VMEM] * 2,
        compiler_params=SMALL,
        name="finish",
    )(parts, proj_col)


def body(corner, edge_row, source_row, proj_row, edge_col, source_col, proj_col):
    lefts, rights = lax.axis_size("left"), lax.axis_size("right")
    rings = lefts // 4

    def bring(turn, swap):
        pairs = []
        for ring in range(rings):
            for low in range(4):
                pairs.append((ring * 4 + low, (ring + turn) % rings * 4 + (low ^ (2 * swap))))
        return lax.ppermute(corner, "left", pairs)

    came = {hop: bring(*hop) for hop in HOPS}
    edge_row = load(edge_row)
    came[HOPS[-1]], edge_row = lax.optimization_barrier((came[HOPS[-1]], edge_row))
    owns, others = [], []
    for far in (1, 0):
        blocks = [came[turn, far] if turn or far else corner for turn in range(rings)]
        owns.insert(0, join(blocks))
        others.insert(0, lax.ppermute(owns[0], "left", [(i, i ^ 1) for i in range(lefts)]))
    held = jnp.concatenate(owns + others, axis=0)

    outs = row_partial(source_row.T, held, edge_row)
    came = [flip(outs[2 * part], ORDERS[part][0], rights) for part in range(3)]
    ours = meet(outs[1::2], came, 0)
    came = [flip(ours[part], ORDERS[part][1], rights) for part in range(3)]
    ours = meet(ours, came, 2)
    came = [flip(ours[part], ORDERS[part][2], rights) for part in range(3)]
    absorbed, *parts = absorb(ours, came, proj_row)

    came = [flip(parts[part], ORDERS[part][0], rights) for part in range(3)]
    edge_col = load(edge_col)
    pieces = [value for pair in zip(parts, came) for value in pair]
    partial_cols = col_partial(source_col, pieces, edge_col, lefts)
    col_parts = lax.all_to_all(partial_cols, "left", 0, 0, tiled=True)
    return absorbed, finish(col_parts, proj_col)


def solution(mesh):
    in_specs = (
        P(("left", "right"), None, None),
        P("left", "right", None, None),
        P("left", "right"),
        P("left", None, None),
        P("right", "left", None, None),
        P("right", "left"),
        P("right", None, None),
    )
    out_specs = (P(("left", "right"), None, None), P("right", "left", None))
    return jax.shard_map(body, mesh=mesh, in_specs=in_specs, out_specs=out_specs, check_vma=False)
```
